256 devices in a mesh: row: 16 (over y_hi, x, core), col: 16 (over z, y_lo).
Axes of the slice: x: 4, y: 4 (y_hi: 2, y_lo: 2; y = y_hi * 2 + y_lo), z: 8, core: 2. Of those that a mesh axis runs over, the one named last changes fastest.
Arguments:
- attn_context: bfloat16 [8192, 4096], P('row', 'col'), may hold values from -6 to 6
- residual: bfloat16 [8192, 2048], P('row', 'col'), may hold values from -8 to 8
- w_out: bfloat16 [4096, 2048], P('col'), may hold values from -0.09375 to 0.09375
- gain_post: bfloat16 [2048], replicated, may hold values from 0.5 to 1.5
- gain_input: bfloat16 [2048], replicated, may hold values from 0.5 to 1.5
- routes: int32 [8192, 8], P('row'), may hold values from 0 to 127, all different within a row; in each aligned block of 512 rows (0 to 511, 512 to 1023, ...) at most 64 rows name the same one
- router_scores: float32 [8192, 8], P('row'), may hold values from 0.02 to 1
- w_gate: bfloat16 [256, 2048, 384], P(('row', 'col')), may hold values from -0.125 to 0.125
- w_up: bfloat16 [256, 2048, 384], P(('row', 'col')), may hold values from -0.125 to 0.125
- w_down: bfloat16 [256, 384, 2048], P(('row', 'col')), may hold values from -0.21875 to 0.21875
- w_query: bfloat16 [2048, 4096], P(None, 'col'), may hold values from -1 to 1
- w_keyval: bfloat16 [2048, 1024], P(None, 'col'), may hold values from -1 to 1
- segment_ids: int32 [16, 504], P('row'), may hold values from 0 to 3, never falling along the last dimension, each value on 1 to 252 neighbouring positions
- cache_lengths: int32 [128], P('row'), may hold values from 1 to 1024, 65536 in all
- holders: int32 [128], P('row'), may hold values from 0 to 127, each once
- cache_keys: bfloat16 [128, 1024, 512], P('row', 'col'), may hold values from -12 to 12
- cache_values: bfloat16 [128, 1024, 512], P('row', 'col'), may hold values from -12 to 12
Outputs:
- hidden_out: bfloat16 [8192, 2048], P('row', 'col')
- new_cache: bfloat16 [8192, 1024], P('row', 'col')
- attention_out: bfloat16 [8192, 4096], P('row', 'col')
The draws below stay inside these ranges and needn't reach their ends.
Inputs may be any that keep to these rules, and one draw needn't show every extreme that they name: `routes`: in the 512 rows of one index of row, no expert is named by more than 64 rows, and in every draw some expert is named by exactly 64. `segment_ids`: each prompt has at most 252 rows and one has exactly that many. `cache_lengths`: the lengths sum to 65536 and the largest is 1024. `holders`: each cache entry belongs to exactly one decode row.
All inputs are finite; a program needn't handle non-finite values. No bound on the sum of `cache_lengths` on one device may be relied on, other than what follows from the above.
Results may differ from the reference program's by a relative error of at most 0.0175.
Values may be sent and summed in bfloat16 or wider, within the bound.
A program may use at most 128 MiB of HBM per device.

```python
import math
import jax
import jax.numpy as jnp
import numpy as np
from jax import lax

D = 2048
FF = 768
TOP = 8
QH = 32
KVH = 4
HD = 128
TOK_DEV = 512
DEC_DEV = 8
LMAX = 1024
EXPERTS = 128
HALF = 384
CAP = 64
PRE_DEV = 504
TOKENS = 8192
CACHES = 128
N_ROW = 16


def draw_residual(key, part):
    noise_rows = jax.random.truncated_normal(jax.random.fold_in(key, 101), -6.0, 6.0, (TOKENS, D), jnp.float32)
    return noise_rows.astype(jnp.bfloat16)


def draw_w_query(key, part):
    weight_scale = D ** (-0.5)
    values = weight_scale * jax.random.truncated_normal(jax.random.fold_in(key, 102), -4.0, 4.0, (D, QH * HD), jnp.float32)
    return values.astype(jnp.bfloat16)


def draw_w_keyval(key, part):
    weight_scale = D ** (-0.5)
    values = weight_scale * jax.random.truncated_normal(jax.random.fold_in(key, 103), -4.0, 4.0, (D, 2 * KVH * HD), jnp.float32)
    return values.astype(jnp.bfloat16)


def draw_cache_keys(key, part):
    values = jax.random.truncated_normal(jax.random.fold_in(key, 104), -6.0, 6.0, (CACHES, LMAX, KVH * HD), jnp.float32)
    return values.astype(jnp.bfloat16)


def draw_cache_values(key, part):
    place = jnp.arange(LMAX).astype(jnp.float32) / LMAX
    channel_sign = jnp.where(jax.random.bernoulli(jax.random.fold_in(key, 211), 0.5, (KVH * HD,)), 1.0, -1.0).astype(jnp.float32)
    noise = jax.random.truncated_normal(jax.random.fold_in(key, 105), -3.0, 3.0, (CACHES, LMAX, KVH * HD), jnp.float32)
    rise = 1.0 + 2.0 * place
    drift = 1.5
    values = noise * rise[None, :, None] + drift * place[None, :, None] * channel_sign[None, None, :]
    return jnp.clip(values, -12.0, 12.0).astype(jnp.bfloat16)


def steps_of(rng, shape, split, smallest, high):
    gain, own = 1.0, jax.random.fold_in(rng, 6)
    for dim, blocks in split:
        draws = jnp.exp(jax.random.uniform(jax.random.fold_in(own, dim), (blocks,), jnp.float32, smallest / len(split), high / len(split)))
        gain = gain * jnp.repeat(draws, shape[dim] // blocks).reshape([-1 if axis == dim else 1 for axis in range(len(shape))])
    return gain


def length_profile(number_of, total, reach, slope):
    weights = [(1 << 20) // math.isqrt(standing ** slope) + 1 for standing in range(2, number_of + 1)]
    surplus, given = total - reach - (number_of - 1), [1] * (number_of - 1)
    while surplus > 0:
        movable = [i for i in range(number_of - 1) if given[i] < reach]
        whole, remaining = sum([weights[i] for i in movable]), surplus
        for i in movable:
            extra = min(reach - given[i], max(1, remaining * weights[i] // whole), surplus)
            given[i] = given[i] + extra
            surplus = surplus - extra
    return np.array([reach] + given)


def uneven_parts(stream_key, amount, total, bound, lean):
    if amount == 2:
        one = jax.random.randint(stream_key, (), max(1, total - bound), min(bound, total - 1) + 1)
        return jnp.stack([one, total - one])
    sizes = jnp.asarray(length_profile(amount, total, bound, lean), jnp.int32)
    couples = (amount - 1) // 2
    donor, taker = sizes[1:1 + 2 * couples:2], sizes[2:2 + 2 * couples:2]
    slack = jnp.minimum(donor - 1, bound - taker)
    passed = jax.random.randint(jax.random.fold_in(stream_key, 1), (couples,), 0, 1 << 20) % (slack + 1)
    sizes = sizes.at[1:1 + 2 * couples:2].set(donor - passed).at[2:2 + 2 * couples:2].set(taker + passed)
    return sizes[jax.random.permutation(jax.random.fold_in(stream_key, 2), amount)]


def assign_block(own_key, own, number, rows, count, top, reach, skew):
    ranking = jax.random.permutation(own_key, count)
    heavy_load, ordinary = load_shares(count, rows * top, reach, skew, True), load_shares(count, rows * top, reach, skew, False)
    places = jnp.arange(count)

    def named(sizes, rotation):
        used = int((sizes > 0).sum())
        fixed = max(1, used // 4)
        moved = fixed + (places - fixed + rotation * (used - fixed)) % max(1, count - fixed)
        return jnp.zeros((count,), jnp.int32).at[ranking[jnp.where(places < fixed, places, moved)]].set(jnp.asarray(sizes, jnp.int32))

    sizes = jnp.where(number % 4 == 0, named(heavy_load, number // 4), named(ordinary, number - number // 4 - 1))
    mixed = jax.random.permutation(jax.random.fold_in(own, 3), count)
    source_of, taker = mixed[0:count // 2 * 2:2], mixed[1:count // 2 * 2:2]
    slack = jnp.minimum(sizes[source_of] - 1, reach - sizes[taker]) // 2
    slack = jnp.where((source_of == ranking[0]) | (taker == ranking[0]) | (sizes[taker] == 0), 0, jnp.maximum(slack, 0))
    moved = jax.random.randint(jax.random.fold_in(own, 4), (count // 2,), 0, 1 << 20) % (slack + 1)
    sizes = sizes.at[source_of].add(-moved).at[taker].add(moved)
    labels = jnp.searchsorted(jnp.cumsum(sizes), jnp.arange(rows * top), side="right").astype(jnp.int32)
    table = labels.reshape(top, rows).T
    table = table[jax.random.permutation(jax.random.fold_in(own, 1), rows)]
    rotation = jax.random.randint(jax.random.fold_in(own, 2), (rows, 1), 0, top)
    return jnp.take_along_axis(table, (jnp.arange(top)[None, :] + rotation) % top, axis=1)


def load_shares(amount, total, reach, slope, full):
    weights = [(1 << 20) // math.isqrt(standing ** slope) + 1 for standing in range(1, amount + 1)]
    largest = reach if full else min(reach, max(-(-total // amount), total * weights[0] // sum(weights)))
    least = 1 if total - largest >= amount - 1 else 0
    given, rest = [largest] + [least] * (amount - 1), total - largest - least * (amount - 1)
    while rest > 0:
        free = [i for i in range(1, amount) if given[i] < largest] or [i for i in range(1, amount) if given[i] < reach]
        pool, left = sum([weights[i] for i in free]), rest
        for i in free:
            addition = min(reach - given[i], max(1, left * weights[i] // pool), rest)
            given[i] = given[i] + addition
            rest = rest - addition
    return np.array(given)


def gaussian(key, dims, scale, reach, pieces=(), held_as=jnp.bfloat16):
    factor_of = steps_of(key, dims, pieces, -0.22, 0.18) if pieces else 1.0
    entries = jax.random.normal(key, dims, jnp.float32) * scale * factor_of
    return jnp.minimum(jnp.maximum(entries, -reach), reach).astype(held_as)


def setup_inputs(seed: int = 0) -> dict:
    streams_of = jax.random.split(jax.random.key(seed), 18)
    attn_context = gaussian(streams_of[0], (TOKENS, QH * HD), 1.0, 6.0, ((0, 16), (1, 16)))
    residual = draw_residual(jax.random.fold_in(streams_of[17], 71), 0)
    w_out = gaussian(streams_of[2], (QH * HD, D), (QH * HD) ** -0.5, 0.09375, ((0, 16),))
    gain_post = jnp.clip(1.0 + 0.1 * jax.random.normal(streams_of[3], (D,), jnp.float32), 0.5, 1.5).astype(jnp.bfloat16)
    gain_input = jnp.clip(1.0 + 0.1 * jax.random.normal(streams_of[4], (D,), jnp.float32), 0.5, 1.5).astype(jnp.bfloat16)
    routes_keys = jax.random.split(jax.random.fold_in(streams_of[5], 1), TOKENS // TOK_DEV)
    routes_turns = jax.random.permutation(jax.random.fold_in(streams_of[5], 3), TOKENS // TOK_DEV)
    routes = jax.vmap(lambda own, number: assign_block(jax.random.fold_in(streams_of[5], 2), own, number, TOK_DEV, EXPERTS, TOP, CAP, 2))(routes_keys, routes_turns).reshape((TOKENS, TOP))
    router_scores = jnp.clip(jnp.exp(math.log(1.0) - 3.912023 * jax.random.uniform(streams_of[6], (TOKENS, TOP), jnp.float32) ** steps_of(streams_of[6], (TOKENS, TOP), ((0, 16),), -0.2, 0.2)), 0.02, 1.0)
    w_gate = gaussian(streams_of[7], (2 * EXPERTS, D, HALF), D ** -0.5, 0.125, ((0, 256),))
    w_up = gaussian(streams_of[8], (2 * EXPERTS, D, HALF), D ** -0.5, 0.125, ((0, 256),))
    w_down = gaussian(streams_of[9], (2 * EXPERTS, HALF, D), FF ** -0.5, 0.21875, ((0, 256),))
    w_query = draw_w_query(jax.random.fold_in(streams_of[17], 71), 0)
    w_keyval = draw_w_keyval(jax.random.fold_in(streams_of[17], 71), 0)
    segment_ids = jax.vmap(lambda own: jnp.searchsorted(jnp.cumsum(uneven_parts(own, 4, PRE_DEV, PRE_DEV // 2, 2)), jnp.arange(PRE_DEV), side="right"))(jax.random.split(streams_of[12], N_ROW)).reshape((N_ROW, PRE_DEV)).astype(jnp.int32)
    cache_lengths = uneven_parts(streams_of[13], CACHES, CACHES * LMAX // 2, LMAX, 2).astype(jnp.int32)
    holders = jax.random.permutation(streams_of[14], CACHES).astype(jnp.int32)
    cache_keys = draw_cache_keys(jax.random.fold_in(streams_of[17], 71), 0)
    cache_values = draw_cache_values(jax.random.fold_in(streams_of[17], 71), 0)
    return dict(attn_context=attn_context, residual=residual, w_out=w_out, gain_post=gain_post, gain_input=gain_input, routes=routes, router_scores=router_scores, w_gate=w_gate, w_up=w_up, w_down=w_down, w_query=w_query, w_keyval=w_keyval, segment_ids=segment_ids, cache_lengths=cache_lengths, holders=holders, cache_keys=cache_keys, cache_values=cache_values)


EPSILON = 1e-06
ROPE_THETA = 1000000.0
NEGATIVE = -1e+30

def rms_norm(hidden, gain_vector):
    values = hidden.astype(jnp.float32)
    inverse = lax.rsqrt(lax.optimization_barrier(jnp.mean(values * values, axis=-1, keepdims=True)) + EPSILON)
    return (values * inverse * gain_vector.astype(jnp.float32)).astype(jnp.bfloat16)

def rotate(values, positions):
    head_width = values.shape[-1]
    half_width = head_width // 2
    indices = jnp.arange(half_width).astype(jnp.float32)
    inverse = ROPE_THETA ** (-2.0 * indices / head_width)
    angles = positions.astype(jnp.float32)[:, None] * inverse[None, :]
    cosine = jnp.concatenate([jnp.cos(angles), jnp.cos(angles)], axis=-1)[:, None, :]
    sine_part = jnp.concatenate([jnp.sin(angles), jnp.sin(angles)], axis=-1)[:, None, :]
    floats = values.astype(jnp.float32)
    turned = jnp.concatenate([-floats[..., half_width:], floats[..., :half_width]], axis=-1)
    return (floats * cosine + turned * sine_part).astype(jnp.bfloat16)

def segment_positions(segment_rows):
    earlier = lax.optimization_barrier(jnp.sum((segment_rows[None, :] < segment_rows[:, None]).astype(jnp.int32), axis=1))
    return jnp.arange(segment_rows.shape[0], dtype=jnp.int32) - earlier.astype(jnp.int32)

def prefill_group(items):
    queries, key_rows, value_rows, segment_rows = items
    count_rows = queries.shape[0]
    grouped = queries.astype(jnp.float32).reshape(count_rows, KVH, QH // KVH, HD)
    scores = jnp.einsum('igqd,jgd->gqij', grouped, key_rows.astype(jnp.float32)) * HD ** (-0.5)
    ordinal = jnp.arange(count_rows)
    allowed = (segment_rows[:, None] == segment_rows[None, :]) & (ordinal[None, :] <= ordinal[:, None])
    scores = jnp.where(allowed, scores, NEGATIVE)
    highest = lax.optimization_barrier(jnp.max(scores, axis=-1, keepdims=True))
    exponent = jnp.exp(scores - highest)
    probability = (exponent / lax.optimization_barrier(jnp.sum(exponent, axis=-1, keepdims=True))).astype(jnp.bfloat16)
    blended = jnp.einsum('gqij,jgd->igqd', probability.astype(jnp.float32), value_rows.astype(jnp.float32))
    return blended.reshape(count_rows, QH * HD).astype(jnp.bfloat16)

def reference(attn_context, residual, w_out, gain_post, gain_input, routes, router_scores, w_gate, w_up, w_down, w_query, w_keyval, segment_ids, cache_lengths, holders, cache_keys, cache_values):
    projected = jnp.dot(attn_context, w_out, preferred_element_type=jnp.float32)
    hidden_mid = (residual.astype(jnp.float32) + projected).astype(jnp.bfloat16)
    normed = rms_norm(hidden_mid, gain_post)
    route_weight = router_scores / lax.optimization_barrier(jnp.sum(router_scores, axis=1, keepdims=True))
    expert_ids = jnp.arange(EXPERTS, dtype=jnp.int32)
    counts = jnp.zeros((TOKENS, EXPERTS), jnp.int32)
    for choice_index in range(TOP):
        counts = counts + (routes[:, choice_index][:, None] == expert_ids[None, :]).astype(jnp.int32)
    grouped_counts = counts.reshape(N_ROW, TOK_DEV, EXPERTS)
    before = (jnp.cumsum(grouped_counts, axis=1) - grouped_counts).reshape(TOKENS, EXPERTS)
    rank = jnp.take_along_axis(before, routes, axis=1)
    group_of = (jnp.arange(TOKENS, dtype=jnp.int32) // TOK_DEV)[:, None]
    slot_index = (group_of * CAP + rank).astype(jnp.int32)
    token_ids = jnp.broadcast_to(jnp.arange(TOKENS, dtype=jnp.int32)[:, None], (TOKENS, TOP))
    table = jnp.full((EXPERTS, N_ROW * CAP), TOKENS, jnp.int32).at[routes, slot_index].set(token_ids)
    weight_table = jnp.zeros((EXPERTS, N_ROW * CAP), jnp.float32).at[routes, slot_index].set(route_weight)
    padded = jnp.concatenate([normed, jnp.zeros((1, D), jnp.bfloat16)], axis=0)

    def expert_step(total, items):
        index_rows, weight_rows, gate_pair, up_pair, down_pair = items
        chosen = padded[index_rows]
        summed = jnp.zeros((index_rows.shape[0], D), jnp.float32)
        for half_index in range(2):
            gate_part = jnp.dot(chosen, gate_pair[half_index], preferred_element_type=jnp.float32)
            up_part = jnp.dot(chosen, up_pair[half_index], preferred_element_type=jnp.float32)
            inner = (jax.nn.silu(gate_part) * up_part).astype(jnp.bfloat16)
            rounded = jnp.dot(inner, down_pair[half_index], preferred_element_type=jnp.float32).astype(jnp.bfloat16)
            summed = summed + lax.optimization_barrier(rounded).astype(jnp.float32)
        return (total.at[index_rows].add(weight_rows[:, None] * summed, mode='drop'), None)
    moe, _ = lax.scan(expert_step, jnp.zeros((TOKENS, D), jnp.float32), (table, weight_table, w_gate.reshape(EXPERTS, 2, D, HALF), w_up.reshape(EXPERTS, 2, D, HALF), w_down.reshape(EXPERTS, 2, HALF, D)))
    hidden_out = (hidden_mid.astype(jnp.float32) + moe).astype(jnp.bfloat16)
    x_in = rms_norm(hidden_out, gain_input)
    query = jnp.dot(x_in, w_query, preferred_element_type=jnp.float32).astype(jnp.bfloat16).reshape(TOKENS, QH, HD)
    keyval = jnp.dot(x_in, w_keyval, preferred_element_type=jnp.float32).astype(jnp.bfloat16).reshape(TOKENS, KVH, 2, HD)
    prompt_pos = jax.vmap(segment_positions)(segment_ids)
    position = jnp.concatenate([cache_lengths.reshape(N_ROW, DEC_DEV), prompt_pos], axis=1).reshape(TOKENS)
    query_rot = rotate(query, position)
    key_rot = rotate(keyval[:, :, 0, :], position)
    value_rows = keyval[:, :, 1, :]
    new_cache = jnp.stack([key_rot, value_rows], axis=2).reshape(TOKENS, 2 * KVH * HD)
    query_grid = query_rot.reshape(N_ROW, TOK_DEV, QH, HD)
    key_grid = key_rot.reshape(N_ROW, TOK_DEV, KVH, HD)
    value_grid = value_rows.reshape(N_ROW, TOK_DEV, KVH, HD)
    prompt_out = lax.map(prefill_group, (query_grid[:, DEC_DEV:], key_grid[:, DEC_DEV:], value_grid[:, DEC_DEV:], segment_ids))

    def decode_one(items):
        single_query, key_new, value_new, length, cache_index = items
        held_keys = cache_keys[cache_index].astype(jnp.float32).reshape(LMAX, KVH, HD)
        held_values = cache_values[cache_index].astype(jnp.float32).reshape(LMAX, KVH, HD)
        grouped = single_query.astype(jnp.float32).reshape(KVH, QH // KVH, HD)
        scores = jnp.einsum('gqd,tgd->gqt', grouped, held_keys) * HD ** (-0.5)
        valid = (jnp.arange(LMAX) < length)[None, None, :]
        scores = jnp.where(valid, scores, NEGATIVE)
        own_score = jnp.einsum('gqd,gd->gq', grouped, key_new.astype(jnp.float32)) * HD ** (-0.5)
        highest = jnp.maximum(lax.optimization_barrier(jnp.max(scores, axis=-1)), own_score)
        exponent = jnp.where(valid, jnp.exp(scores - highest[..., None]), 0.0)
        own_exp = jnp.exp(own_score - highest)
        total = lax.optimization_barrier(jnp.sum(exponent, axis=-1)) + own_exp
        blended = jnp.einsum('gqt,tgd->gqd', exponent, held_values, precision=lax.Precision.HIGHEST)
        blended = blended + own_exp[..., None] * value_new.astype(jnp.float32)[:, None, :]
        return (blended / total[..., None]).reshape(QH * HD).astype(jnp.bfloat16)
    decode_out = lax.map(decode_one, (query_grid[:, :DEC_DEV].reshape(CACHES, QH, HD), key_grid[:, :DEC_DEV].reshape(CACHES, KVH, HD), value_grid[:, :DEC_DEV].reshape(CACHES, KVH, HD), cache_lengths, holders))
    attention_out = jnp.concatenate([decode_out.reshape(N_ROW, DEC_DEV, QH * HD), prompt_out], axis=1).reshape(TOKENS, QH * HD)
    return (hidden_out, new_cache, attention_out)
```

```python
import functools

import jax
import jax.numpy as jnp
from jax import lax
from jax.experimental import pallas as pl
from jax.experimental.pallas import tpu as pltpu
from jax.sharding import PartitionSpec as P

TOP = 8
QH = 32
KVH = 4
HD = 128
EPSILON = 1e-06
ROPE_THETA = 1000000.0
NEGATIVE = -1e30
MESH = pl.DeviceIdType.MESH

D = 2048
HALF_D = 1024
LEFT = pl.ds(0, HALF_D)
RIGHT = pl.ds(HALF_D, HALF_D)
ROWS = 512
BLOCK = 32
CAP = 64
RING_SEMS = 23
TILE = 512


def remote(src, dst, send, recv, index, device):
    return pltpu.make_async_remote_copy(
        src_ref=src,
        dst_ref=dst,
        send_sem=send.at[index],
        recv_sem=recv.at[index],
        device_id=device,
        device_id_type=MESH,
    )


def around():
    row = lax.axis_index("row")
    col = lax.axis_index("col")
    z = col // 2
    y = lax.rem(col, 2)
    after = (row, lax.rem(z + 1, 8) * 2 + y)
    before = (row, lax.rem(z + 7, 8) * 2 + y)
    beside = (row, z * 2 + 1 - y)
    return z, y, after, before, beside


def reduce_blocks(place, blocks, y_left, up_left, down_left, up_right, down_right, y_right, send, recv, base):
    z, y, after, before, beside = place
    other = 1 - y
    started = []

    def go(src, dst, index, device):
        copy = remote(src, dst, send, recv, base + index, device)
        copy.start()
        started.append(copy)
        return copy

    def at(offset):
        return lax.rem(z + offset + 8, 8)

    crossing = {}
    for index, offset in enumerate((4, -3, 3, -2, 2, -1, 1, 0)):
        t = at(offset)
        crossing[offset] = go(blocks.at[other, t, :, LEFT], y_left.at[t], index, beside)
    up_l, down_l, up_r, down_r = [], [], [], []
    for step in range(4):
        if step < 3:
            t = at(3 - step)
            if step:
                up_r[-1].wait_recv()
                blocks[:, t, :, RIGHT] = (
                    blocks[:, t, :, RIGHT].astype(jnp.float32) + up_right[step - 1].astype(jnp.float32)
                ).astype(jnp.bfloat16)
            up_r.append(go(blocks.at[:, t, :, RIGHT], up_right.at[step], 8 + step, after))
        t = at(step - 4)
        if step:
            down_r[-1].wait_recv()
            blocks[:, t, :, RIGHT] = (
                blocks[:, t, :, RIGHT].astype(jnp.float32) + down_right[step - 1].astype(jnp.float32)
            ).astype(jnp.bfloat16)
        down_r.append(go(blocks.at[:, t, :, RIGHT], down_right.at[step], 11 + step, before))
        t = at(4 - step)
        crossing[4 - step].wait_recv()
        value = blocks[y, t, :, LEFT].astype(jnp.float32) + y_left[t].astype(jnp.float32)
        if step:
            up_l[-1].wait_recv()
            value = value + up_left[step - 1].astype(jnp.float32)
        blocks[y, t, :, LEFT] = value.astype(jnp.bfloat16)
        up_l.append(go(blocks.at[y, t, :, LEFT], up_left.at[step], 15 + step, after))
        if step < 3:
            t = at(step - 3)
            crossing[step - 3].wait_recv()
            value = blocks[y, t, :, LEFT].astype(jnp.float32) + y_left[t].astype(jnp.float32)
            if step:
                down_l[-1].wait_recv()
                value = value + down_left[step - 1].astype(jnp.float32)
            blocks[y, t, :, LEFT] = value.astype(jnp.bfloat16)
            down_l.append(go(blocks.at[y, t, :, LEFT], down_left.at[step], 19 + step, before))
    up_r[-1].wait_recv()
    down_r[-1].wait_recv()
    blocks[other, z, :, RIGHT] = (
        blocks[other, z, :, RIGHT].astype(jnp.float32)
        + up_right[2, other].astype(jnp.float32)
        + down_right[3, other].astype(jnp.float32)
    ).astype(jnp.bfloat16)
    last = go(blocks.at[other, z, :, RIGHT], y_right, 22, beside)
    right = (
        blocks[y, z, :, RIGHT].astype(jnp.float32)
        + up_right[2, y].astype(jnp.float32)
        + down_right[3, y].astype(jnp.float32)
    )
    crossing[0].wait_recv()
    up_l[-1].wait_recv()
    down_l[-1].wait_recv()
    left = (
        blocks[y, z, :, LEFT].astype(jnp.float32)
        + y_left[z].astype(jnp.float32)
        + up_left[3].astype(jnp.float32)
        + down_left[2].astype(jnp.float32)
    )
    last.wait_recv()
    right = right + y_right[...].astype(jnp.float32)
    return left, right, started


def gather_blocks(place, full, send, recv, base):
    z, y, after, before, beside = place
    started = []

    def go(view, index, device):
        copy = remote(view, view, send, recv, base + index, device)
        copy.start()
        started.append(copy)
        return copy

    def at(offset):
        return lax.rem(z + offset + 8, 8)

    first = go(full.at[z, y, :, RIGHT], 0, beside)
    crossing = []
    up_l, down_l, up_r, down_r = [], [], [], []

    def cross(t):
        crossing.append(go(full.at[t, y, :, LEFT], 1 + len(crossing), beside))

    for step in range(4):
        if step:
            up_l[-1].wait_recv()
        up_l.append(go(full.at[at(-step), y, :, LEFT], 9 + step, after))
        if step < 3:
            if step:
                down_l[-1].wait_recv()
            down_l.append(go(full.at[at(step), y, :, LEFT], 13 + step, before))
        if step == 0:
            first.wait_recv()
        if step < 3:
            if step:
                up_r[-1].wait_recv()
            up_r.append(go(full.at[at(-step), :, :, RIGHT], 16 + step, after))
        if step:
            down_r[-1].wait_recv()
        down_r.append(go(full.at[at(step), :, :, RIGHT], 19 + step, before))
        cross(at(-step))
        if 0 < step < 3:
            cross(at(step))
    down_l[-1].wait_recv()
    cross(at(3))
    up_l[-1].wait_recv()
    cross(at(-4))
    up_r[-1].wait_recv()
    down_r[-1].wait_recv()
    for copy in crossing:
        copy.wait_recv()
    return started


def ring_scratch():
    return [
        pltpu.VMEM((2, 8, BLOCK, D), jnp.bfloat16),
        pltpu.VMEM((8, BLOCK, HALF_D), jnp.bfloat16),
        pltpu.VMEM((4, BLOCK, HALF_D), jnp.bfloat16),
        pltpu.VMEM((3, BLOCK, HALF_D), jnp.bfloat16),
        pltpu.VMEM((3, 2, BLOCK, HALF_D), jnp.bfloat16),
        pltpu.VMEM((4, 2, BLOCK, HALF_D), jnp.bfloat16),
        pltpu.VMEM((BLOCK, HALF_D), jnp.bfloat16),
    ]


def greet(devices):
    barrier = pltpu.get_barrier_semaphore()
    for device in devices:
        pl.semaphore_signal(barrier, inc=1, device_id=device, device_id_type=MESH)
    return barrier


def by_block(value):
    return value.reshape(8, 2, BLOCK, value.shape[-1])


def out_kernel(context, w_out, residual, gain, normed, mid, blocks, *rest):
    buffers, (send, recv) = rest[:6], rest[6:]
    place = around()
    z, y, after, before, beside = place
    barrier = greet((after, before, beside))
    for tile in range(0, D, TILE):
        columns = pl.ds(tile, TILE)
        value = by_block(
            jnp.dot(context[...], w_out[:, columns], preferred_element_type=jnp.float32).astype(jnp.bfloat16)
        )
        blocks[0, :, :, columns] = value[:, 0]
        blocks[1, :, :, columns] = value[:, 1]
    own = pl.ds(pl.multiple_of((z * 2 + y) * 128, 128), 128)
    value = jnp.dot(context[...], w_out[:, own], preferred_element_type=jnp.float32)
    value = by_block((value + residual[...].astype(jnp.float32)).astype(jnp.bfloat16))
    blocks[0, :, :, own] = value[:, 0]
    blocks[1, :, :, own] = value[:, 1]
    pl.semaphore_wait(barrier, 3)
    left, right, started = reduce_blocks(place, blocks, *buffers, send, recv, 0)
    left = left.astype(jnp.bfloat16)
    right = right.astype(jnp.bfloat16)
    mid[:, :HALF_D] = left
    mid[:, HALF_D:] = right
    left = left.astype(jnp.float32)
    right = right.astype(jnp.float32)
    mean = (
        jnp.sum(left * left, axis=-1, keepdims=True) + jnp.sum(right * right, axis=-1, keepdims=True)
    ) * (1.0 / D)
    inverse = lax.rsqrt(mean + EPSILON)
    gains = gain[...].astype(jnp.float32)
    normed[z, y, :, LEFT] = (left * inverse * gains[:, :HALF_D]).astype(jnp.bfloat16)
    normed[z, y, :, RIGHT] = (right * inverse * gains[:, HALF_D:]).astype(jnp.bfloat16)
    started = started + gather_blocks(place, normed, send, recv, RING_SEMS)
    for copy in started:
        copy.wait_send()


def out_project(context, w_out, residual, gain):
    vmem = pl.BlockSpec(memory_space=pltpu.VMEM)
    return pl.pallas_call(
        out_kernel,
        out_shape=(
            jax.ShapeDtypeStruct((8, 2, BLOCK, D), jnp.bfloat16),
            jax.ShapeDtypeStruct((BLOCK, D), jnp.bfloat16),
        ),
        in_specs=[vmem] * 4,
        out_specs=(vmem, vmem),
        scratch_shapes=ring_scratch()
        + [pltpu.SemaphoreType.DMA((2 * RING_SEMS,)), pltpu.SemaphoreType.DMA((2 * RING_SEMS,))],
        compiler_params=pltpu.CompilerParams(
            collective_id=0, has_side_effects=True, vmem_limit_bytes=40 << 20
        ),
        name="out_project",
    )(context, w_out, residual, gain.reshape(1, D))


GROUPS = (8, 12, 4, 0)


def expert_kernel(
    normed, routes, scores, w_gate, w_up, w_down, mid, full, share,
    blocks, y_left, up_left, down_left, up_right, down_right, y_right,
    going, coming, back, total, weights, send, recv,
):
    row = lax.axis_index("row")
    place = around()
    z, y, after, before, beside = place
    yh, x, core = row // 8, lax.rem(row // 2, 4), lax.rem(row, 2)

    def partner(o, sign):
        a, b, d = o // 8, (o // 2) % 4, o % 2
        there = lax.rem(yh + a, 2) * 8 + lax.rem(x + sign * b + 4, 4) * 2 + lax.rem(core + d, 2)
        return (there, z * 2 + lax.rem(y + a, 2))

    partners = [partner(o, 1) for o in range(1, 16)]
    barrier = greet([after, before, beside] + partners)
    offsets = lax.broadcasted_iota(jnp.int32, (16, 1), 0)
    a, b, d = offsets // 8, lax.rem(offsets // 2, 4), lax.rem(offsets, 2)
    expert = (
        lax.rem(yh + a, 2) * 8 + lax.rem(x + b, 4) * 2 + lax.rem(core + d, 2)
    ) * 8 + z
    score = scores[...]
    share_of = score / jnp.sum(score, axis=0, keepdims=True)
    hit = jnp.zeros((16, ROWS), jnp.float32)
    weight = jnp.zeros((16, ROWS), jnp.float32)
    for choice in range(TOP):
        match = routes[choice : choice + 1, :] == expert
        hit = hit + jnp.where(match, 1.0, 0.0)
        weight = weight + jnp.where(match, share_of[choice : choice + 1, :], 0.0)
    earlier = lax.broadcasted_iota(jnp.int32, (ROWS, ROWS), 0) < lax.broadcasted_iota(
        jnp.int32, (ROWS, ROWS), 1
    )
    rank = jnp.dot(
        hit.astype(jnp.bfloat16),
        jnp.where(earlier, 1.0, 0.0).astype(jnp.bfloat16),
        preferred_element_type=jnp.float32,
    )
    rank = jnp.where(hit > 0.0, rank, -1.0).astype(jnp.int32)
    slots = lax.broadcasted_iota(jnp.int32, (CAP, ROWS), 0)
    pl.semaphore_wait(barrier, 18)
    started = []
    arrivals = {}
    for group in GROUPS:
        picks = []
        for o in range(group, group + 4):
            chosen = slots == rank[o : o + 1, :]
            picks.append(jnp.where(chosen, 1.0, 0.0).astype(jnp.bfloat16))
            weights[o * CAP : (o + 1) * CAP, :] = jnp.where(chosen, weight[o : o + 1, :], 0.0).astype(
                jnp.bfloat16
            )
        pick = jnp.concatenate(picks, axis=0)
        for tile in range(0, D, TILE):
            columns = pl.ds(tile, TILE)
            value = jnp.dot(pick, normed[:, columns], preferred_element_type=jnp.float32)
            value = value.astype(jnp.bfloat16).reshape(4, CAP, TILE)
            if group:
                going[group : group + 4, :, columns] = value
            else:
                coming[0, :, columns] = value[0]
                going[1:4, :, columns] = value[1:]
        for o in range(max(group, 1), group + 4):
            copy = remote(going.at[o], coming.at[o], send, recv, o, partner(o, 1))
            copy.start()
            started.append(copy)
            arrivals[o] = copy
    returns = {}
    for group in GROUPS:
        for o in range(max(group, 1), group + 4):
            arrivals[o].wait_recv()
        rows = coming[group : group + 4].reshape(4 * CAP, D)
        gate = jnp.dot(rows, w_gate[...], preferred_element_type=jnp.float32)
        up = jnp.dot(rows, w_up[...], preferred_element_type=jnp.float32)
        inner = (gate / (1.0 + jnp.exp(-gate)) * up).astype(jnp.bfloat16)
        for tile in range(0, D, TILE):
            columns = pl.ds(tile, TILE)
            value = jnp.dot(inner, w_down[:, columns], preferred_element_type=jnp.float32)
            coming[group : group + 4, :, columns] = value.astype(jnp.bfloat16).reshape(4, CAP, TILE)
        for o in range(max(group, 1), group + 4):
            copy = remote(coming.at[o], back.at[o], send, recv, 16 + o, partner(o, -1))
            copy.start()
            started.append(copy)
            returns[o] = copy
    back[0] = coming[0]
    for index, group in enumerate(GROUPS[::-1]):
        for o in range(max(group, 1), group + 4):
            returns[o].wait_recv()
        spread = weights[group * CAP : (group + 4) * CAP, :]
        for tile in range(0, D, TILE):
            columns = pl.ds(tile, TILE)
            value = lax.dot_general(
                spread,
                back[group : group + 4, :, columns].reshape(4 * CAP, TILE),
                (((0,), (0,)), ((), ())),
                preferred_element_type=jnp.float32,
            )
            if index:
                value = value + total[:, columns]
            if index < 3:
                total[:, columns] = value
            else:
                value = by_block(value.astype(jnp.bfloat16))
                blocks[0, :, :, columns] = value[:, 0]
                blocks[1, :, :, columns] = value[:, 1]
    left, right, ring = reduce_blocks(
        place, blocks, y_left, up_left, down_left, up_right, down_right, y_right, send, recv, 32
    )
    full[z, y, :, LEFT] = (mid[:, :HALF_D].astype(jnp.float32) + left).astype(jnp.bfloat16)
    full[z, y, :, RIGHT] = (mid[:, HALF_D:].astype(jnp.float32) + right).astype(jnp.bfloat16)
    started = started + ring + gather_blocks(place, full, send, recv, 32 + RING_SEMS)
    own = pl.ds(pl.multiple_of((z * 2 + y) * 128, 128), 128)
    share[...] = full[:, :, :, own].reshape(ROWS, 128)
    for copy in started:
        copy.wait_send()


def experts(normed, routes, scores, w_gate, w_up, w_down, mid):
    vmem = pl.BlockSpec(memory_space=pltpu.VMEM)
    sems = 32 + 2 * RING_SEMS
    return pl.pallas_call(
        expert_kernel,
        out_shape=(
            jax.ShapeDtypeStruct((8, 2, BLOCK, D), jnp.bfloat16),
            jax.ShapeDtypeStruct((ROWS, 128), jnp.bfloat16),
        ),
        in_specs=[vmem] * 7,
        out_specs=(vmem, vmem),
        scratch_shapes=ring_scratch()
        + [
            pltpu.VMEM((16, CAP, D), jnp.bfloat16),
            pltpu.VMEM((16, CAP, D), jnp.bfloat16),
            pltpu.VMEM((16, CAP, D), jnp.bfloat16),
            pltpu.VMEM((ROWS, D), jnp.float32),
            pltpu.VMEM((16 * CAP, ROWS), jnp.bfloat16),
            pltpu.SemaphoreType.DMA((sems,)),
            pltpu.SemaphoreType.DMA((sems,)),
        ],
        compiler_params=pltpu.CompilerParams(
            collective_id=1, has_side_effects=True, vmem_limit_bytes=52 << 20
        ),
        name="experts",
    )(normed, routes, scores, w_gate, w_up, w_down, mid)


def merged_2(value, axis, join):
    pieces = jax.tree.map(lambda part: lax.all_gather(part, axis), value)
    head = jax.tree.map(lambda part: part[0], pieces)
    tail = jax.tree.map(lambda part: part[1:], pieces)
    running, _ = lax.scan(lambda running, share: (join(running, share), None), head, tail)
    return running


def rms_norm(hidden, gain_vector):
    values = hidden.astype(jnp.float32)
    inverse = lax.rsqrt(jnp.mean(values * values, axis=-1, keepdims=True) + EPSILON)
    return (values * inverse * gain_vector.astype(jnp.float32)).astype(jnp.bfloat16)


def rotate(values, positions):
    head_width = values.shape[-1]
    half_width = head_width // 2
    indices = jnp.arange(half_width).astype(jnp.float32)
    inverse = ROPE_THETA ** (-2.0 * indices / head_width)
    angles = positions.astype(jnp.float32)[:, None] * inverse[None, :]
    cosine = jnp.concatenate([jnp.cos(angles), jnp.cos(angles)], axis=-1)[:, None, :]
    sine_part = jnp.concatenate([jnp.sin(angles), jnp.sin(angles)], axis=-1)[:, None, :]
    floats = values.astype(jnp.float32)
    turned = jnp.concatenate([-floats[..., half_width:], floats[..., :half_width]], axis=-1)
    return (floats * cosine + turned * sine_part).astype(jnp.bfloat16)


def segment_positions(segment_rows):
    earlier = jnp.sum((segment_rows[None, :] < segment_rows[:, None]).astype(jnp.int32), axis=1)
    return jnp.arange(segment_rows.shape[0], dtype=jnp.int32) - earlier


def join_partials(first, second):
    highest = jnp.maximum(first[0], second[0])
    factor_one = jnp.exp(first[0] - highest)
    factor_two = jnp.exp(second[0] - highest)
    weight_mass = first[1] * factor_one + second[1] * factor_two
    accum_out = first[2] * factor_one[..., None] + second[2] * factor_two[..., None]
    return (highest, weight_mass, accum_out)


def shards(
    attn_context,
    residual,
    w_out,
    gain_post,
    gain_input,
    routes,
    router_scores,
    w_gate,
    w_up,
    w_down,
    w_query,
    w_keyval,
    segment_ids,
    cache_lengths,
    holders,
    cache_keys,
    cache_values,
):
    col_index = lax.axis_index("col")
    col_count = lax.axis_size("col")
    row_count = lax.axis_size("row")
    tok_rows = attn_context.shape[0]
    normed, mid = out_project(attn_context, w_out, residual, gain_post)
    full, hidden_out = experts(
        normed.reshape(tok_rows, D),
        routes.T,
        router_scores.T,
        w_gate[0],
        w_up[0],
        w_down[0],
        mid,
    )
    x_in = rms_norm(full.reshape(tok_rows, D), gain_input)
    heads_local = QH // col_count
    dec_count = cache_lengths.shape[0]
    score_scale = HD ** (-0.5)
    query_local = (
        jnp.dot(x_in, w_query, preferred_element_type=jnp.float32)
        .astype(jnp.bfloat16)
        .reshape(tok_rows, heads_local, HD)
    )
    keyval_local = jnp.dot(x_in, w_keyval, preferred_element_type=jnp.float32).astype(jnp.bfloat16)
    position = jnp.concatenate([cache_lengths, segment_positions(segment_ids[0])], axis=0)
    query_rot = rotate(query_local, position)
    dec_query = query_rot[:dec_count].reshape(dec_count, heads_local * HD)
    keyval_all, payload = (
        lax.all_gather(keyval_local, "col", axis=1, tiled=True),
        lax.all_gather(dec_query, "col", axis=1, tiled=True),
    )
    keyval_heads = keyval_all.reshape(tok_rows, KVH, 2, HD)
    key_rot = rotate(keyval_heads[:, :, 0, :], position)
    value_rows = keyval_heads[:, :, 1, :]
    cache_full = jnp.stack([key_rot, value_rows], axis=2).reshape(tok_rows, 2 * KVH * HD)
    cache_share = cache_full.shape[1] // col_count
    new_cache = lax.dynamic_slice_in_dim(cache_full, col_index * cache_share, cache_share, 1)
    head_kv = col_index * heads_local // (QH // KVH)
    my_keys = lax.dynamic_index_in_dim(key_rot, head_kv, 1, keepdims=False)
    my_values = lax.dynamic_index_in_dim(value_rows, head_kv, 1, keepdims=False)
    prompt_query = query_rot[dec_count:]
    prompt_keys = my_keys[dec_count:]
    prompt_values = my_values[dec_count:]
    prompt_rows = prompt_query.shape[0]
    scores = (
        jnp.einsum("ihd,jd->hij", prompt_query, prompt_keys, preferred_element_type=jnp.float32)
        * score_scale
    )
    ordinal = jnp.arange(prompt_rows)
    segment_rows = segment_ids[0]
    allowed = (segment_rows[:, None] == segment_rows[None, :]) & (
        ordinal[None, :] <= ordinal[:, None]
    )
    scores = jnp.where(allowed[None, :, :], scores, NEGATIVE)
    highest = jnp.max(scores, axis=-1, keepdims=True)
    exponent = jnp.exp(scores - highest)
    probability = (exponent / jnp.sum(exponent, axis=-1, keepdims=True)).astype(jnp.bfloat16)
    prompt_out = jnp.einsum(
        "hij,jd->ihd", probability, prompt_values, preferred_element_type=jnp.float32
    )
    prompt_out = prompt_out.astype(jnp.bfloat16).reshape(prompt_rows, heads_local * HD)
    holder_dev = holders // dec_count
    holder_slot = holders % dec_count
    outbox = (
        jnp.zeros((row_count, dec_count, payload.shape[1]), jnp.bfloat16)
        .at[holder_dev, holder_slot]
        .set(payload)
    )
    length_box = (
        jnp.zeros((row_count, dec_count), jnp.int32).at[holder_dev, holder_slot].set(cache_lengths)
    )
    inbox, length_in = (
        lax.all_to_all(outbox, "row", split_axis=0, concat_axis=0, tiled=True),
        lax.all_to_all(length_box, "row", split_axis=0, concat_axis=0, tiled=True),
    )
    slot_query = jnp.sum(inbox.astype(jnp.float32), axis=0).astype(jnp.bfloat16)
    slot_length = jnp.sum(length_in, axis=0)
    span_len = cache_keys.shape[1]
    span_start = col_index * span_len
    grouped = slot_query.reshape(dec_count, KVH, QH // KVH, HD)
    held_keys = cache_keys.reshape(dec_count, span_len, KVH, HD)
    held_values = cache_values.reshape(dec_count, span_len, KVH, HD).astype(jnp.float32)
    held_scores = (
        jnp.einsum("sgqd,stgd->sgqt", grouped, held_keys, preferred_element_type=jnp.float32)
        * score_scale
    )
    valid = ((span_start + jnp.arange(span_len))[None, :] < slot_length[:, None])[:, None, None, :]
    held_scores = jnp.where(valid, held_scores, NEGATIVE)
    score_top = jnp.max(held_scores, axis=-1)
    held_exp = jnp.where(valid, jnp.exp(held_scores - score_top[..., None]), 0.0)
    weight_mass = jnp.sum(held_exp, axis=-1).reshape(dec_count, QH)
    accum_out = jnp.einsum(
        "sgqt,stgd->sgqd", held_exp, held_values, precision=lax.Precision.HIGHEST
    ).reshape(dec_count, QH, HD)
    score_top = score_top.reshape(dec_count, QH)
    merged = merged_2((score_top, weight_mass, accum_out), "col", join_partials)
    part_top = lax.dynamic_slice_in_dim(merged[0], col_index * heads_local, heads_local, 1)
    part_mass = lax.dynamic_slice_in_dim(merged[1], col_index * heads_local, heads_local, 1)
    part_accum = lax.dynamic_slice_in_dim(merged[2], col_index * heads_local, heads_local, 1)
    reply_top = jnp.broadcast_to(part_top[None], (row_count,) + part_top.shape)
    reply_mass = jnp.broadcast_to(part_mass[None], (row_count,) + part_mass.shape)
    reply_accum = jnp.broadcast_to(part_accum[None], (row_count,) + part_accum.shape)
    back_top, back_mass, back_accum = (
        lax.all_to_all(reply_top, "row", split_axis=0, concat_axis=0, tiled=True),
        lax.all_to_all(reply_mass, "row", split_axis=0, concat_axis=0, tiled=True),
        lax.all_to_all(reply_accum, "row", split_axis=0, concat_axis=0, tiled=True),
    )
    remote_top = back_top[holder_dev, holder_slot]
    remote_mass = back_mass[holder_dev, holder_slot]
    remote_accum = back_accum[holder_dev, holder_slot]
    own_query = query_rot[:dec_count].astype(jnp.float32)
    own_key = my_keys[:dec_count].astype(jnp.float32)
    own_value = my_values[:dec_count].astype(jnp.float32)
    own_score = (
        jnp.einsum("shd,sd->sh", own_query, own_key, precision=lax.Precision.HIGHEST) * score_scale
    )
    final_top = jnp.maximum(remote_top, own_score)
    remote_factor = jnp.exp(remote_top - final_top)
    own_factor = jnp.exp(own_score - final_top)
    numerator = (
        remote_accum * remote_factor[..., None] + own_factor[..., None] * own_value[:, None, :]
    )
    denominator = remote_mass * remote_factor + own_factor
    decode_out = (
        (numerator / denominator[..., None])
        .reshape(dec_count, heads_local * HD)
        .astype(jnp.bfloat16)
    )
    attention_out = jnp.concatenate([decode_out, prompt_out], axis=0)
    return (hidden_out, new_cache, attention_out)


def solution(mesh):
    return jax.shard_map(
        shards,
        mesh=mesh,
        in_specs=(
            P("row", "col"),
            P("row", "col"),
            P("col", None),
            P(),
            P(),
            P("row", None),
            P("row", None),
            P(("row", "col"), None, None),
            P(("row", "col"), None, None),
            P(("row", "col"), None, None),
            P(None, "col"),
            P(None, "col"),
            P("row", None),
            P("row"),
            P("row"),
            P("row", "col", None),
            P("row", "col", None),
        ),
        out_specs=(P("row", "col"), P("row", "col"), P("row", "col")),
        check_vma=False,
    )
```

```python
import functools

import jax
import jax.numpy as jnp
from jax import lax
from jax.experimental import pallas as pl
from jax.experimental.pallas import tpu as pltpu
from jax.sharding import PartitionSpec as P

TOP = 8
QH = 32
KVH = 4
HD = 128
EPSILON = 1e-06
ROPE_THETA = 1000000.0
NEGATIVE = -1e30
MESH = pl.DeviceIdType.MESH

D = 2048
HALF_D = 1024
LEFT = pl.ds(0, HALF_D)
RIGHT = pl.ds(HALF_D, HALF_D)
ROWS = 512
BLOCK = 32
CAP = 64
RING_SEMS = 23
TILE = 512


def remote(src, dst, send, recv, index, device):
    return pltpu.make_async_remote_copy(
        src_ref=src,
        dst_ref=dst,
        send_sem=send.at[index],
        recv_sem=recv.at[index],
        device_id=device,
        device_id_type=MESH,
    )


def around():
    row = lax.axis_index("row")
    col = lax.axis_index("col")
    z = col // 2
    y = lax.rem(col, 2)
    after = (row, lax.rem(z + 1, 8) * 2 + y)
    before = (row, lax.rem(z + 7, 8) * 2 + y)
    beside = (row, z * 2 + 1 - y)
    return z, y, after, before, beside


def reduce_blocks(place, blocks, y_left, up_left, down_left, up_right, down_right, y_right, send, recv, base):
    z, y, after, before, beside = place
    other = 1 - y
    started = []

    def go(src, dst, index, device):
        copy = remote(src, dst, send, recv, base + index, device)
        copy.start()
        started.append(copy)
        return copy

    def at(offset):
        return lax.rem(z + offset + 8, 8)

    crossing = {}
    for index, offset in enumerate((4, -3, 3, -2, 2, -1, 1, 0)):
        t = at(offset)
        crossing[offset] = go(blocks.at[other, t, :, LEFT], y_left.at[t], index, beside)
    up_l, down_l, up_r, down_r = [], [], [], []
    for step in range(4):
        if step < 3:
            t = at(3 - step)
            if step:
                up_r[-1].wait_recv()
                blocks[:, t, :, RIGHT] = (
                    blocks[:, t, :, RIGHT].astype(jnp.float32) + up_right[step - 1].astype(jnp.float32)
                ).astype(jnp.bfloat16)
            up_r.append(go(blocks.at[:, t, :, RIGHT], up_right.at[step], 8 + step, after))
        t = at(step - 4)
        if step:
            down_r[-1].wait_recv()
            blocks[:, t, :, RIGHT] = (
                blocks[:, t, :, RIGHT].astype(jnp.float32) + down_right[step - 1].astype(jnp.float32)
            ).astype(jnp.bfloat16)
        down_r.append(go(blocks.at[:, t, :, RIGHT], down_right.at[step], 11 + step, before))
        t = at(4 - step)
        crossing[4 - step].wait_recv()
        value = blocks[y, t, :, LEFT].astype(jnp.float32) + y_left[t].astype(jnp.float32)
        if step:
            up_l[-1].wait_recv()
            value = value + up_left[step - 1].astype(jnp.float32)
        blocks[y, t, :, LEFT] = value.astype(jnp.bfloat16)
        up_l.append(go(blocks.at[y, t, :, LEFT], up_left.at[step], 15 + step, after))
        if step < 3:
            t = at(step - 3)
            crossing[step - 3].wait_recv()
            value = blocks[y, t, :, LEFT].astype(jnp.float32) + y_left[t].astype(jnp.float32)
            if step:
                down_l[-1].wait_recv()
                value = value + down_left[step - 1].astype(jnp.float32)
            blocks[y, t, :, LEFT] = value.astype(jnp.bfloat16)
            down_l.append(go(blocks.at[y, t, :, LEFT], down_left.at[step], 19 + step, before))
    up_r[-1].wait_recv()
    down_r[-1].wait_recv()
    blocks[other, z, :, RIGHT] = (
        blocks[other, z, :, RIGHT].astype(jnp.float32)
        + up_right[2, other].astype(jnp.float32)
        + down_right[3, other].astype(jnp.float32)
    ).astype(jnp.bfloat16)
    last = go(blocks.at[other, z, :, RIGHT], y_right, 22, beside)
    right = (
        blocks[y, z, :, RIGHT].astype(jnp.float32)
        + up_right[2, y].astype(jnp.float32)
        + down_right[3, y].astype(jnp.float32)
    )
    crossing[0].wait_recv()
    up_l[-1].wait_recv()
    down_l[-1].wait_recv()
    left = (
        blocks[y, z, :, LEFT].astype(jnp.float32)
        + y_left[z].astype(jnp.float32)
        + up_left[3].astype(jnp.float32)
        + down_left[2].astype(jnp.float32)
    )
    last.wait_recv()
    right = right + y_right[...].astype(jnp.float32)
    return left, right, started


def gather_blocks(place, full, send, recv, base):
    z, y, after, before, beside = place
    started = []

    def go(view, index, device):
        copy = remote(view, view, send, recv, base + index, device)
        copy.start()
        started.append(copy)
        return copy

    def at(offset):
        return lax.rem(z + offset + 8, 8)

    first = go(full.at[z, y, :, RIGHT], 0, beside)
    crossing = []
    up_l, down_l, up_r, down_r = [], [], [], []

    def cross(t):
        crossing.append(go(full.at[t, y, :, LEFT], 1 + len(crossing), beside))

    for step in range(4):
        if step:
            up_l[-1].wait_recv()
        up_l.append(go(full.at[at(-step), y, :, LEFT], 9 + step, after))
        if step < 3:
            if step:
                down_l[-1].wait_recv()
            down_l.append(go(full.at[at(step), y, :, LEFT], 13 + step, before))
        if step == 0:
            first.wait_recv()
        if step < 3:
            if step:
                up_r[-1].wait_recv()
            up_r.append(go(full.at[at(-step), :, :, RIGHT], 16 + step, after))
        if step:
            down_r[-1].wait_recv()
        down_r.append(go(full.at[at(step), :, :, RIGHT], 19 + step, before))
        cross(at(-step))
        if 0 < step < 3:
            cross(at(step))
    down_l[-1].wait_recv()
    cross(at(3))
    up_l[-1].wait_recv()
    cross(at(-4))
    up_r[-1].wait_recv()
    down_r[-1].wait_recv()
    for copy in crossing:
        copy.wait_recv()
    return started


def ring_scratch():
    return [
        pltpu.VMEM((2, 8, BLOCK, D), jnp.bfloat16),
        pltpu.VMEM((8, BLOCK, HALF_D), jnp.bfloat16),
        pltpu.VMEM((4, BLOCK, HALF_D), jnp.bfloat16),
        pltpu.VMEM((3, BLOCK, HALF_D), jnp.bfloat16),
        pltpu.VMEM((3, 2, BLOCK, HALF_D), jnp.bfloat16),
        pltpu.VMEM((4, 2, BLOCK, HALF_D), jnp.bfloat16),
        pltpu.VMEM((BLOCK, HALF_D), jnp.bfloat16),
    ]


def greet(devices):
    barrier = pltpu.get_barrier_semaphore()
    for device in devices:
        pl.semaphore_signal(barrier, inc=1, device_id=device, device_id_type=MESH)
    return barrier


def by_block(value):
    return value.reshape(8, 2, BLOCK, value.shape[-1])


def out_kernel(context, w_out, residual, gain, normed, mid, blocks, *rest):
    buffers, (send, recv) = rest[:6], rest[6:]
    place = around()
    z, y, after, before, beside = place
    barrier = greet((after, before, beside))
    for tile in range(0, D, TILE):
        columns = pl.ds(tile, TILE)
        value = by_block(
            jnp.dot(context[...], w_out[:, columns], preferred_element_type=jnp.float32).astype(jnp.bfloat16)
        )
        blocks[0, :, :, columns] = value[:, 0]
        blocks[1, :, :, columns] = value[:, 1]
    own = pl.ds(pl.multiple_of((z * 2 + y) * 128, 128), 128)
    value = jnp.dot(context[...], w_out[:, own], preferred_element_type=jnp.float32)
    value = by_block((value + residual[...].astype(jnp.float32)).astype(jnp.bfloat16))
    blocks[0, :, :, own] = value[:, 0]
    blocks[1, :, :, own] = value[:, 1]
    pl.semaphore_wait(barrier, 3)
    left, right, started = reduce_blocks(place, blocks, *buffers, send, recv, 0)
    left = left.astype(jnp.bfloat16)
    right = right.astype(jnp.bfloat16)
    mid[:, :HALF_D] = left
    mid[:, HALF_D:] = right
    left = left.astype(jnp.float32)
    right = right.astype(jnp.float32)
    mean = (
        jnp.sum(left * left, axis=-1, keepdims=True) + jnp.sum(right * right, axis=-1, keepdims=True)
    ) * (1.0 / D)
    inverse = lax.rsqrt(mean + EPSILON)
    gains = gain[...].astype(jnp.float32)
    normed[z, y, :, LEFT] = (left * inverse * gains[:, :HALF_D]).astype(jnp.bfloat16)
    normed[z, y, :, RIGHT] = (right * inverse * gains[:, HALF_D:]).astype(jnp.bfloat16)
    started = started + gather_blocks(place, normed, send, recv, RING_SEMS)
    for copy in started:
        copy.wait_send()


def out_project(context, w_out, residual, gain):
    vmem = pl.BlockSpec(memory_space=pltpu.VMEM)
    return pl.pallas_call(
        out_kernel,
        out_shape=(
            jax.ShapeDtypeStruct((8, 2, BLOCK, D), jnp.bfloat16),
            jax.ShapeDtypeStruct((BLOCK, D), jnp.bfloat16),
        ),
        in_specs=[vmem] * 4,
        out_specs=(vmem, vmem),
        scratch_shapes=ring_scratch()
        + [pltpu.SemaphoreType.DMA((2 * RING_SEMS,)), pltpu.SemaphoreType.DMA((2 * RING_SEMS,))],
        compiler_params=pltpu.CompilerParams(
            collective_id=0, has_side_effects=True, vmem_limit_bytes=40 << 20
        ),
        name="out_project",
    )(context, w_out, residual, gain.reshape(1, D))


GROUPS = (8, 12, 4, 0)
TABLE_SEMS = 32 + 2 * RING_SEMS


def expert_kernel(
    normed, routes, scores, w_gate, w_up, w_down, mid, table, full, share, tables,
    blocks, y_left, up_left, down_left, up_right, down_right, y_right,
    going, coming, back, total, weights, listed, send, recv,
):
    row = lax.axis_index("row")
    place = around()
    z, y, after, before, beside = place
    yh, x, core = row // 8, lax.rem(row // 2, 4), lax.rem(row, 2)

    def partner(o, sign):
        a, b, d = o // 8, (o // 2) % 4, o % 2
        there = lax.rem(yh + a, 2) * 8 + lax.rem(x + sign * b + 4, 4) * 2 + lax.rem(core + d, 2)
        return (there, z * 2 + lax.rem(y + a, 2))

    partners = [partner(o, 1) for o in range(1, 16)]
    barrier = greet([after, before, beside] + partners)
    offsets = lax.broadcasted_iota(jnp.int32, (16, 1), 0)
    a, b, d = offsets // 8, lax.rem(offsets // 2, 4), lax.rem(offsets, 2)
    expert = (
        lax.rem(yh + a, 2) * 8 + lax.rem(x + b, 4) * 2 + lax.rem(core + d, 2)
    ) * 8 + z
    score = scores[...]
    share_of = score / jnp.sum(score, axis=0, keepdims=True)
    hit = jnp.zeros((16, ROWS), jnp.float32)
    weight = jnp.zeros((16, ROWS), jnp.float32)
    for choice in range(TOP):
        match = routes[choice : choice + 1, :] == expert
        hit = hit + jnp.where(match, 1.0, 0.0)
        weight = weight + jnp.where(match, share_of[choice : choice + 1, :], 0.0)
    earlier = lax.broadcasted_iota(jnp.int32, (ROWS, ROWS), 0) < lax.broadcasted_iota(
        jnp.int32, (ROWS, ROWS), 1
    )
    rank = jnp.dot(
        hit.astype(jnp.bfloat16),
        jnp.where(earlier, 1.0, 0.0).astype(jnp.bfloat16),
        preferred_element_type=jnp.float32,
    )
    rank = jnp.where(hit > 0.0, rank, -1.0).astype(jnp.int32)
    slots = lax.broadcasted_iota(jnp.int32, (CAP, ROWS), 0)
    pl.semaphore_wait(barrier, 18)
    started = []
    arrivals = {}
    lists = []
    for o in range(1, 16):
        copy = remote(table, listed.at[o], send, recv, TABLE_SEMS + o, partner(o, 1))
        copy.start()
        lists.append(copy)
    for group in GROUPS:
        picks = []
        for o in range(group, group + 4):
            chosen = slots == rank[o : o + 1, :]
            picks.append(jnp.where(chosen, 1.0, 0.0).astype(jnp.bfloat16))
            weights[o * CAP : (o + 1) * CAP, :] = jnp.where(chosen, weight[o : o + 1, :], 0.0).astype(
                jnp.bfloat16
            )
        pick = jnp.concatenate(picks, axis=0)
        for tile in range(0, D, TILE):
            columns = pl.ds(tile, TILE)
            value = jnp.dot(pick, normed[:, columns], preferred_element_type=jnp.float32)
            value = value.astype(jnp.bfloat16).reshape(4, CAP, TILE)
            if group:
                going[group : group + 4, :, columns] = value
            else:
                coming[0, :, columns] = value[0]
                going[1:4, :, columns] = value[1:]
        for o in range(max(group, 1), group + 4):
            copy = remote(going.at[o], coming.at[o], send, recv, o, partner(o, 1))
            copy.start()
            started.append(copy)
            arrivals[o] = copy
    returns = {}
    for group in GROUPS:
        for o in range(max(group, 1), group + 4):
            arrivals[o].wait_recv()
        rows = coming[group : group + 4].reshape(4 * CAP, D)
        gate = jnp.dot(rows, w_gate[...], preferred_element_type=jnp.float32)
        up = jnp.dot(rows, w_up[...], preferred_element_type=jnp.float32)
        inner = (gate / (1.0 + jnp.exp(-gate)) * up).astype(jnp.bfloat16)
        for tile in range(0, D, TILE):
            columns = pl.ds(tile, TILE)
            value = jnp.dot(inner, w_down[:, columns], preferred_element_type=jnp.float32)
            coming[group : group + 4, :, columns] = value.astype(jnp.bfloat16).reshape(4, CAP, TILE)
        for o in range(max(group, 1), group + 4):
            copy = remote(coming.at[o], back.at[o], send, recv, 16 + o, partner(o, -1))
            copy.start()
            started.append(copy)
            returns[o] = copy
    back[0] = coming[0]
    for copy in lists:
        copy.wait_recv()
    known = table[...]
    for o in range(1, 16):
        known = known + listed[o]
    tables[...] = known
    for index, group in enumerate(GROUPS[::-1]):
        for o in range(max(group, 1), group + 4):
            returns[o].wait_recv()
        spread = weights[group * CAP : (group + 4) * CAP, :]
        for tile in range(0, D, TILE):
            columns = pl.ds(tile, TILE)
            value = lax.dot_general(
                spread,
                back[group : group + 4, :, columns].reshape(4 * CAP, TILE),
                (((0,), (0,)), ((), ())),
                preferred_element_type=jnp.float32,
            )
            if index:
                value = value + total[:, columns]
            if index < 3:
                total[:, columns] = value
            else:
                value = by_block(value.astype(jnp.bfloat16))
                blocks[0, :, :, columns] = value[:, 0]
                blocks[1, :, :, columns] = value[:, 1]
    left, right, ring = reduce_blocks(
        place, blocks, y_left, up_left, down_left, up_right, down_right, y_right, send, recv, 32
    )
    full[z, y, :, LEFT] = (mid[:, :HALF_D].astype(jnp.float32) + left).astype(jnp.bfloat16)
    full[z, y, :, RIGHT] = (mid[:, HALF_D:].astype(jnp.float32) + right).astype(jnp.bfloat16)
    started = started + lists + ring + gather_blocks(place, full, send, recv, 32 + RING_SEMS)
    own = pl.ds(pl.multiple_of((z * 2 + y) * 128, 128), 128)
    share[...] = full[:, :, :, own].reshape(ROWS, 128)
    for copy in started:
        copy.wait_send()


def experts(normed, routes, scores, w_gate, w_up, w_down, mid, table):
    vmem = pl.BlockSpec(memory_space=pltpu.VMEM)
    sems = TABLE_SEMS + 16
    return pl.pallas_call(
        expert_kernel,
        out_shape=(
            jax.ShapeDtypeStruct((8, 2, BLOCK, D), jnp.bfloat16),
            jax.ShapeDtypeStruct((ROWS, 128), jnp.bfloat16),
            jax.ShapeDtypeStruct((8, 128), jnp.int32),
        ),
        in_specs=[vmem] * 8,
        out_specs=(vmem, vmem, vmem),
        scratch_shapes=ring_scratch()
        + [
            pltpu.VMEM((16, CAP, D), jnp.bfloat16),
            pltpu.VMEM((16, CAP, D), jnp.bfloat16),
            pltpu.VMEM((16, CAP, D), jnp.bfloat16),
            pltpu.VMEM((ROWS, D), jnp.float32),
            pltpu.VMEM((16 * CAP, ROWS), jnp.bfloat16),
            pltpu.VMEM((16, 8, 128), jnp.int32),
            pltpu.SemaphoreType.DMA((sems,)),
            pltpu.SemaphoreType.DMA((sems,)),
        ],
        compiler_params=pltpu.CompilerParams(
            collective_id=1, has_side_effects=True, vmem_limit_bytes=52 << 20
        ),
        name="experts",
    )(normed, routes, scores, w_gate, w_up, w_down, mid, table)


SCALE = HD ** (-0.5)
PACK = 384


def turn(value, cosine, sine):
    return value * cosine + pltpu.roll(value, HD // 2, value.ndim - 1) * sine


def stats_of(top, mass, lane):
    return jnp.where(
        lane == 0, top[0], jnp.where(lane == 1, top[1], jnp.where(lane == 2, mass[0], mass[1]))
    )


def attend_kernel(
    full, gain, w_query, w_keyval, cosine, sine, segment_column, segment_row, holders, tables,
    cache_keys, cache_values, new_cache, attention,
    x_in, query, pieces, keys, values, own_query, all_query, slot_query, slots_query,
    parts, parts_in, reply, replies, send, recv,
):
    row = lax.axis_index("row")
    col = lax.axis_index("col")
    quarter = lax.rem(col, 4)
    first = col - quarter

    def along_row(o):
        return (lax.rem(row + o, 16), col)

    def along_col(o):
        return (row, lax.rem(col + o, 16))

    barrier = greet([along_row(o) for o in range(1, 16)] + [along_col(o) for o in range(1, 16)])
    started = []

    def go(src, dst, index, device):
        copy = remote(src, dst, send, recv, index, device)
        copy.start()
        started.append(copy)
        return copy

    gains = gain[...].astype(jnp.float32)

    def norm(value):
        value = value.astype(jnp.float32)
        inverse = lax.rsqrt(jnp.mean(value * value, axis=-1, keepdims=True) + EPSILON)
        return (value * inverse * gains).astype(jnp.bfloat16)

    early = jnp.dot(norm(full[:16, :]), w_query[...], preferred_element_type=jnp.float32)
    early = early.astype(jnp.bfloat16).astype(jnp.float32)
    for head in range(2):
        span = pl.ds(head * HD, HD)
        turned = turn(early[:, head * HD : (head + 1) * HD], cosine[:16, :], sine[:16, :])
        own_query[:, span] = turned.astype(jnp.bfloat16).astype(jnp.float32)[:8]
    all_query[row] = own_query[...]
    pl.semaphore_wait(barrier, 30)
    asks = [go(own_query, all_query.at[row], o, along_row(o)) for o in range(1, 16)]
    for tile in range(0, ROWS, 64):
        x_in[tile : tile + 64, :] = norm(full[tile : tile + 64, :])
    keyval = jnp.dot(x_in[...], w_keyval[...], preferred_element_type=jnp.float32).astype(jnp.bfloat16)
    pieces[quarter] = jnp.concatenate([keyval[: ROWS // 2], keyval[ROWS // 2 :]], axis=1)
    shares = [
        go(pieces.at[quarter], pieces.at[quarter], 16 + o, (row, first + lax.rem(quarter + o, 4)))
        for o in range(1, 4)
    ]
    for copy in asks:
        copy.wait_recv()
    held = (
        tables[0:1, :] == row * 8 + lax.broadcasted_iota(jnp.int32, (8, 128), 0)
    )
    length = jnp.sum(jnp.where(held, tables[1:2, :], 0), axis=1, keepdims=True)
    slot_query[...] = jnp.dot(
        jnp.where(held, 1.0, 0.0).astype(jnp.bfloat16),
        all_query[...].reshape(128, 2 * HD).astype(jnp.bfloat16),
        preferred_element_type=jnp.float32,
    )
    slots_query[col] = slot_query[...]
    tells = [go(slot_query, slots_query.at[col], 20 + o, along_col(o)) for o in range(1, 16)]
    for head in range(2):
        span = pl.ds(head * HD, HD)
        value = jnp.dot(x_in[...], w_query[:, span], preferred_element_type=jnp.float32)
        value = value.astype(jnp.bfloat16).astype(jnp.float32)
        query[:, span] = turn(value, cosine[...], sine[...]).astype(jnp.bfloat16)
    for copy in tells:
        copy.wait_recv()
    group = lax.rem(lax.broadcasted_iota(jnp.int32, (32, 4 * HD), 0), 16) // 4
    matched = group == lax.broadcasted_iota(jnp.int32, (32, 4 * HD), 1) // HD
    spot = col * 64 + lax.broadcasted_iota(jnp.int32, (32, 64), 1)
    lane = lax.broadcasted_iota(jnp.int32, (16, HD), 1)
    for slot in range(8):
        asked = slots_query[:, slot, :]
        asked = jnp.concatenate([asked[:, :HD], asked[:, HD:]], axis=0)
        asked = jnp.where(matched, jnp.concatenate([asked] * 4, axis=1), 0.0).astype(jnp.bfloat16)
        scores = SCALE * lax.dot_general(
            asked, cache_keys[slot], (((1,), (1,)), ((), ())), preferred_element_type=jnp.float32
        )
        valid = spot < length[slot : slot + 1, :]
        scores = jnp.where(valid, scores, NEGATIVE)
        top = jnp.max(scores, axis=1, keepdims=True)
        grown = jnp.where(valid, jnp.exp(scores - top), 0.0)
        mass = jnp.sum(grown, axis=1, keepdims=True)
        blend = jnp.dot(grown.astype(jnp.bfloat16), cache_values[slot], preferred_element_type=jnp.float32)
        blend = jnp.where(matched, blend, 0.0)
        blend = blend[:, :HD] + blend[:, HD : 2 * HD] + blend[:, 2 * HD : 3 * HD] + blend[:, 3 * HD :]
        parts[:, slot, :HD] = blend[:16]
        parts[:, slot, HD : 2 * HD] = blend[16:]
        parts[:, slot, 2 * HD :] = stats_of((top[:16], top[16:]), (mass[:16], mass[16:]), lane)
    parts_in[0] = parts[col]
    sums = [
        go(parts.at[lax.rem(col + o, 16)], parts_in.at[o], 36 + o, along_col(o)) for o in range(1, 16)
    ]
    for copy in shares:
        copy.wait_recv()

    def piece(index):
        value = pieces[index]
        return jnp.concatenate([value[:, : HD // 2], value[:, HD // 2 :]], axis=0)

    quarters = [piece(index) for index in range(4)]
    key = jnp.concatenate(quarters[:2], axis=1).astype(jnp.float32)
    keys[...] = turn(key, cosine[...], sine[...]).astype(jnp.bfloat16)
    values[...] = jnp.concatenate(quarters[2:], axis=1)
    new_cache[...] = jnp.where(
        quarter == 0,
        keys[:, : HD // 2],
        jnp.where(
            quarter == 1,
            keys[:, HD // 2 :],
            jnp.where(quarter == 2, values[:, : HD // 2], values[:, HD // 2 :]),
        ),
    )

    def prompt(head):
        span = pl.ds(head * HD, HD)
        for tile in range(0, ROWS, 128):
            reach = tile + 128
            scores = SCALE * lax.dot_general(
                query[tile:reach, span], keys[:reach, :], (((1,), (1,)), ((), ())),
                preferred_element_type=jnp.float32,
            )
            allowed = (segment_column[tile:reach, :] == segment_row[:, :reach]) & (
                lax.broadcasted_iota(jnp.int32, (128, reach), 1)
                <= lax.broadcasted_iota(jnp.int32, (128, reach), 0) + tile
            )
            scores = jnp.where(allowed, scores, NEGATIVE)
            grown = jnp.exp(scores - jnp.max(scores, axis=1, keepdims=True))
            chance = (grown / jnp.sum(grown, axis=1, keepdims=True)).astype(jnp.bfloat16)
            attention[tile:reach, span] = jnp.dot(
                chance, values[:reach, :], preferred_element_type=jnp.float32
            ).astype(jnp.bfloat16)

    prompt(0)
    for copy in sums:
        copy.wait_recv()
    tops, masses = [], []
    for head in range(2):
        top = parts_in[:, :, 2 * HD + head : 2 * HD + head + 1]
        mass = parts_in[:, :, 2 * HD + 2 + head : 2 * HD + 3 + head]
        highest = jnp.max(top, axis=0)
        factor = jnp.exp(top - highest[None])
        span = pl.ds(head * HD, HD)
        reply[:, span] = jnp.sum(parts_in[:, :, span] * factor, axis=0)
        tops.append(highest)
        masses.append(jnp.sum(mass * factor, axis=0))
    reply[:, 2 * HD :] = stats_of(tops, masses, lane[:8])
    replies[row] = reply[...]
    backs = [go(reply, replies.at[row], 52 + o, along_row(o)) for o in range(1, 16)]
    prompt(1)
    for copy in backs:
        copy.wait_recv()
    mine = jnp.where(holders[...] == lax.broadcasted_iota(jnp.int32, (8, 128), 1), 1.0, 0.0)
    got = jnp.dot(
        mine,
        replies[...].reshape(128, PACK),
        preferred_element_type=jnp.float32,
        precision=lax.Precision.HIGHEST,
    )
    own_key = keys[:16, :].astype(jnp.float32)[:8]
    own_value = values[:16, :].astype(jnp.float32)[:8]
    for head in range(2):
        span = pl.ds(head * HD, HD)
        own = SCALE * jnp.sum(own_query[:, span] * own_key, axis=1, keepdims=True)
        top = got[:, 2 * HD + head : 2 * HD + head + 1]
        mass = got[:, 2 * HD + 2 + head : 2 * HD + 3 + head]
        highest = jnp.maximum(top, own)
        theirs = jnp.exp(top - highest)
        ours = jnp.exp(own - highest)
        result = (got[:, head * HD : (head + 1) * HD] * theirs + own_value * ours) / (mass * theirs + ours)
        result = jnp.concatenate([result, result], axis=0)
        decoded = lax.broadcasted_iota(jnp.int32, (16, HD), 0) < 8
        attention[:16, span] = jnp.where(
            decoded, result, attention[:16, span].astype(jnp.float32)
        ).astype(jnp.bfloat16)
    for copy in started:
        copy.wait_send()


def attend(full, gain, w_query, w_keyval, cosine, sine, segments, holders, tables, cache_keys, cache_values):
    vmem = pl.BlockSpec(memory_space=pltpu.VMEM)
    f32, bf16 = jnp.float32, jnp.bfloat16
    return pl.pallas_call(
        attend_kernel,
        out_shape=(
            jax.ShapeDtypeStruct((ROWS, 64), bf16),
            jax.ShapeDtypeStruct((ROWS, 2 * HD), bf16),
        ),
        in_specs=[vmem] * 12,
        out_specs=(vmem, vmem),
        scratch_shapes=[
            pltpu.VMEM((ROWS, D), bf16),
            pltpu.VMEM((ROWS, 2 * HD), bf16),
            pltpu.VMEM((4, ROWS // 2, HD), bf16),
            pltpu.VMEM((ROWS, HD), bf16),
            pltpu.VMEM((ROWS, HD), bf16),
            pltpu.VMEM((8, 2 * HD), f32),
            pltpu.VMEM((16, 8, 2 * HD), f32),
            pltpu.VMEM((8, 2 * HD), f32),
            pltpu.VMEM((16, 8, 2 * HD), f32),
            pltpu.VMEM((16, 8, PACK), f32),
            pltpu.VMEM((16, 8, PACK), f32),
            pltpu.VMEM((8, PACK), f32),
            pltpu.VMEM((16, 8, PACK), f32),
            pltpu.SemaphoreType.DMA((68,)),
            pltpu.SemaphoreType.DMA((68,)),
        ],
        compiler_params=pltpu.CompilerParams(
            collective_id=2, has_side_effects=True, vmem_limit_bytes=48 << 20
        ),
        name="attend",
    )(
        full, gain.reshape(1, D), w_query, w_keyval, cosine, sine,
        segments.reshape(ROWS, 1), segments.reshape(1, ROWS), holders.reshape(8, 1), tables,
        cache_keys, cache_values,
    )


def shards(
    attn_context,
    residual,
    w_out,
    gain_post,
    gain_input,
    routes,
    router_scores,
    w_gate,
    w_up,
    w_down,
    w_query,
    w_keyval,
    segment_ids,
    cache_lengths,
    holders,
    cache_keys,
    cache_values,
):
    row = lax.axis_index("row")
    segment = segment_ids[0]
    earlier = jnp.sum((segment[None, :] < segment[:, None]).astype(jnp.int32), axis=1)
    position = jnp.concatenate([cache_lengths, jnp.arange(segment.shape[0], dtype=jnp.int32) - earlier])
    indices = jnp.arange(HD // 2).astype(jnp.float32)
    angles = position.astype(jnp.float32)[:, None] * (ROPE_THETA ** (-2.0 * indices / HD))[None, :]
    cosine, sine = jnp.cos(angles), jnp.sin(angles)
    cosine = jnp.concatenate([cosine, cosine], axis=1)
    sine = jnp.concatenate([-sine, sine], axis=1)
    segments = jnp.concatenate([jnp.full((8,), -1, jnp.int32), segment])
    table = jnp.stack([holders, cache_lengths])
    table = jnp.pad(table, ((0, 6), (0, 0)))
    table = jnp.where(
        jnp.arange(128, dtype=jnp.int32)[None, :] // 8 == row, jnp.tile(table, (1, 16)), 0
    )
    normed, mid = out_project(attn_context, w_out, residual, gain_post)
    full, hidden_out, tables = experts(
        normed.reshape(ROWS, D), routes.T, router_scores.T, w_gate[0], w_up[0], w_down[0], mid, table
    )
    new_cache, attention_out = attend(
        full.reshape(ROWS, D), gain_input, w_query, w_keyval, cosine, sine, segments, holders, tables,
        cache_keys, cache_values,
    )
    return (hidden_out, new_cache, attention_out)


def solution(mesh):
    return jax.shard_map(
        shards,
        mesh=mesh,
        in_specs=(
            P("row", "col"),
            P("row", "col"),
            P("col", None),
            P(),
            P(),
            P("row", None),
            P("row", None),
            P(("row", "col"), None, None),
            P(("row", "col"), None, None),
            P(("row", "col"), None, None),
            P(None, "col"),
            P(None, "col"),
            P("row", None),
            P("row"),
            P("row"),
            P("row", "col", None),
            P("row", "col", None),
        ),
        out_specs=(P("row", "col"), P("row", "col"), P("row", "col")),
        check_vma=False,
    )
```

```python
import functools

import jax
import jax.numpy as jnp
from jax import lax
from jax.experimental import pallas as pl
from jax.experimental.pallas import tpu as pltpu
from jax.sharding import PartitionSpec as P

TOP = 8
QH = 32
KVH = 4
HD = 128
EPSILON = 1e-06
ROPE_THETA = 1000000.0
NEGATIVE = -1e30
MESH = pl.DeviceIdType.MESH

D = 2048
HALF_D = 1024
LEFT = pl.ds(0, HALF_D)
RIGHT = pl.ds(HALF_D, HALF_D)
ROWS = 512
BLOCK = 32
CAP = 64
RING_SEMS = 23
TILE = 512


def remote(src, dst, send, recv, index, device):
    return pltpu.make_async_remote_copy(
        src_ref=src,
        dst_ref=dst,
        send_sem=send.at[index],
        recv_sem=recv.at[index],
        device_id=device,
        device_id_type=MESH,
    )


def around():
    row = lax.axis_index("row")
    col = lax.axis_index("col")
    z = col // 2
    y = lax.rem(col, 2)
    after = (row, lax.rem(z + 1, 8) * 2 + y)
    before = (row, lax.rem(z + 7, 8) * 2 + y)
    beside = (row, z * 2 + 1 - y)
    return z, y, after, before, beside


def reduce_blocks(place, blocks, y_left, up_left, down_left, up_right, down_right, y_right, send, recv, base):
    z, y, after, before, beside = place
    other = 1 - y
    started = []

    def go(src, dst, index, device):
        copy = remote(src, dst, send, recv, base + index, device)
        copy.start()
        started.append(copy)
        return copy

    def at(offset):
        return lax.rem(z + offset + 8, 8)

    crossing = {}
    for index, offset in enumerate((4, -3, 3, -2, 2, -1, 1, 0)):
        t = at(offset)
        crossing[offset] = go(blocks.at[other, t, :, LEFT], y_left.at[t], index, beside)
    up_l, down_l, up_r, down_r = [], [], [], []
    for step in range(4):
        if step < 3:
            t = at(3 - step)
            if step:
                up_r[-1].wait_recv()
                blocks[:, t, :, RIGHT] = (
                    blocks[:, t, :, RIGHT].astype(jnp.float32) + up_right[step - 1].astype(jnp.float32)
                ).astype(jnp.bfloat16)
            up_r.append(go(blocks.at[:, t, :, RIGHT], up_right.at[step], 8 + step, after))
        t = at(step - 4)
        if step:
            down_r[-1].wait_recv()
            blocks[:, t, :, RIGHT] = (
                blocks[:, t, :, RIGHT].astype(jnp.float32) + down_right[step - 1].astype(jnp.float32)
            ).astype(jnp.bfloat16)
        down_r.append(go(blocks.at[:, t, :, RIGHT], down_right.at[step], 11 + step, before))
        t = at(4 - step)
        crossing[4 - step].wait_recv()
        value = blocks[y, t, :, LEFT].astype(jnp.float32) + y_left[t].astype(jnp.float32)
        if step:
            up_l[-1].wait_recv()
            value = value + up_left[step - 1].astype(jnp.float32)
        blocks[y, t, :, LEFT] = value.astype(jnp.bfloat16)
        up_l.append(go(blocks.at[y, t, :, LEFT], up_left.at[step], 15 + step, after))
        if step < 3:
            t = at(step - 3)
            crossing[step - 3].wait_recv()
            value = blocks[y, t, :, LEFT].astype(jnp.float32) + y_left[t].astype(jnp.float32)
            if step:
                down_l[-1].wait_recv()
                value = value + down_left[step - 1].astype(jnp.float32)
            blocks[y, t, :, LEFT] = value.astype(jnp.bfloat16)
            down_l.append(go(blocks.at[y, t, :, LEFT], down_left.at[step], 19 + step, before))
    up_r[-1].wait_recv()
    down_r[-1].wait_recv()
    blocks[other, z, :, RIGHT] = (
        blocks[other, z, :, RIGHT].astype(jnp.float32)
        + up_right[2, other].astype(jnp.float32)
        + down_right[3, other].astype(jnp.float32)
    ).astype(jnp.bfloat16)
    last = go(blocks.at[other, z, :, RIGHT], y_right, 22, beside)
    right = (
        blocks[y, z, :, RIGHT].astype(jnp.float32)
        + up_right[2, y].astype(jnp.float32)
        + down_right[3, y].astype(jnp.float32)
    )
    crossing[0].wait_recv()
    up_l[-1].wait_recv()
    down_l[-1].wait_recv()
    left = (
        blocks[y, z, :, LEFT].astype(jnp.float32)
        + y_left[z].astype(jnp.float32)
        + up_left[3].astype(jnp.float32)
        + down_left[2].astype(jnp.float32)
    )
    last.wait_recv()
    right = right + y_right[...].astype(jnp.float32)
    return left, right, started


def gather_blocks(place, full, send, recv, base):
    z, y, after, before, beside = place
    started = []

    def go(view, index, device):
        copy = remote(view, view, send, recv, base + index, device)
        copy.start()
        started.append(copy)
        return copy

    def at(offset):
        return lax.rem(z + offset + 8, 8)

    first = go(full.at[z, y, :, RIGHT], 0, beside)
    crossing = []
    up_l, down_l, up_r, down_r = [], [], [], []

    def cross(t):
        crossing.append(go(full.at[t, y, :, LEFT], 1 + len(crossing), beside))

    for step in range(4):
        if step:
            up_l[-1].wait_recv()
        up_l.append(go(full.at[at(-step), y, :, LEFT], 9 + step, after))
        if step < 3:
            if step:
                down_l[-1].wait_recv()
            down_l.append(go(full.at[at(step), y, :, LEFT], 13 + step, before))
        if step == 0:
            first.wait_recv()
        if step < 3:
            if step:
                up_r[-1].wait_recv()
            up_r.append(go(full.at[at(-step), :, :, RIGHT], 16 + step, after))
        if step:
            down_r[-1].wait_recv()
        down_r.append(go(full.at[at(step), :, :, RIGHT], 19 + step, before))
        cross(at(-step))
        if 0 < step < 3:
            cross(at(step))
    down_l[-1].wait_recv()
    cross(at(3))
    up_l[-1].wait_recv()
    cross(at(-4))
    up_r[-1].wait_recv()
    down_r[-1].wait_recv()
    for copy in crossing:
        copy.wait_recv()
    return started


def ring_scratch():
    return [
        pltpu.VMEM((2, 8, BLOCK, D), jnp.bfloat16),
        pltpu.VMEM((8, BLOCK, HALF_D), jnp.bfloat16),
        pltpu.VMEM((4, BLOCK, HALF_D), jnp.bfloat16),
        pltpu.VMEM((3, BLOCK, HALF_D), jnp.bfloat16),
        pltpu.VMEM((3, 2, BLOCK, HALF_D), jnp.bfloat16),
        pltpu.VMEM((4, 2, BLOCK, HALF_D), jnp.bfloat16),
        pltpu.VMEM((BLOCK, HALF_D), jnp.bfloat16),
    ]


def greet(devices):
    barrier = pltpu.get_barrier_semaphore()
    for device in devices:
        pl.semaphore_signal(barrier, inc=1, device_id=device, device_id_type=MESH)
    return barrier


def by_block(value):
    return value.reshape(8, 2, BLOCK, value.shape[-1])


def fetch(pairs, sems):
    copies = [pltpu.make_async_copy(far, near, sems.at[index]) for index, (far, near) in enumerate(pairs)]
    for copy in copies:
        copy.start()
    return copies


def out_kernel(context, w_out, residual, gain, normed, mid, blocks, *rest):
    buffers, (send, recv) = rest[:6], rest[6:]
    place = around()
    z, y, after, before, beside = place
    barrier = greet((after, before, beside))
    for tile in range(0, D, TILE):
        columns = pl.ds(tile, TILE)
        value = by_block(
            jnp.dot(context[...], w_out[:, columns], preferred_element_type=jnp.float32).astype(jnp.bfloat16)
        )
        blocks[0, :, :, columns] = value[:, 0]
        blocks[1, :, :, columns] = value[:, 1]
    own = pl.ds(pl.multiple_of((z * 2 + y) * 128, 128), 128)
    value = jnp.dot(context[...], w_out[:, own], preferred_element_type=jnp.float32)
    value = by_block((value + residual[...].astype(jnp.float32)).astype(jnp.bfloat16))
    blocks[0, :, :, own] = value[:, 0]
    blocks[1, :, :, own] = value[:, 1]
    pl.semaphore_wait(barrier, 3)
    left, right, started = reduce_blocks(place, blocks, *buffers, send, recv, 0)
    left = left.astype(jnp.bfloat16)
    right = right.astype(jnp.bfloat16)
    mid[:, :HALF_D] = left
    mid[:, HALF_D:] = right
    left = left.astype(jnp.float32)
    right = right.astype(jnp.float32)
    mean = (
        jnp.sum(left * left, axis=-1, keepdims=True) + jnp.sum(right * right, axis=-1, keepdims=True)
    ) * (1.0 / D)
    inverse = lax.rsqrt(mean + EPSILON)
    gains = gain[...].astype(jnp.float32)
    normed[z, y, :, LEFT] = (left * inverse * gains[:, :HALF_D]).astype(jnp.bfloat16)
    normed[z, y, :, RIGHT] = (right * inverse * gains[:, HALF_D:]).astype(jnp.bfloat16)
    started = started + gather_blocks(place, normed, send, recv, RING_SEMS)
    for copy in started:
        copy.wait_send()


def out_project(context, w_out, residual, gain):
    vmem = pl.BlockSpec(memory_space=pltpu.VMEM)
    return pl.pallas_call(
        out_kernel,
        out_shape=(
            jax.ShapeDtypeStruct((8, 2, BLOCK, D), jnp.bfloat16),
            jax.ShapeDtypeStruct((BLOCK, D), jnp.bfloat16),
        ),
        in_specs=[vmem] * 4,
        out_specs=(vmem, vmem),
        scratch_shapes=ring_scratch()
        + [pltpu.SemaphoreType.DMA((2 * RING_SEMS,)), pltpu.SemaphoreType.DMA((2 * RING_SEMS,))],
        compiler_params=pltpu.CompilerParams(
            collective_id=0, has_side_effects=True, vmem_limit_bytes=40 << 20
        ),
        name="out_project",
    )(context, w_out, residual, gain.reshape(1, D))


SPLIT = (4, 5, 10, 11, 12, 13, 14, 15)
SENDS = (12, 14, 2, 10, 4, 6, 8, 0)
PLAN = (
    ('pass', (12, 13, 14, 15)),
    ('work', (0,)),
    ('pass', (10, 11)),
    ('work', (12,)),
    ('pass', (4, 5)),
    ('work', (8,)),
    ('give', (12, 13, 14, 15)),
    ('work', (4,)),
    ('give', (10, 11, 4, 5)),
)
WHOLE_RUNS = ((0, 4), (6, 10))
SPLIT_RUNS = ((10, 12), (12, 16), (4, 6))
SHARE_SEMS = 32
SWAP_SEMS = 48
RING_BASE = 64
TABLE_SEMS = RING_BASE + 2 * RING_SEMS


def expert_kernel(
    normed, routes, scores, far_gate, far_up, far_down, mid, table, full, share, tables,
    blocks, y_left, up_left, down_left, up_right, down_right, y_right,
    going, coming, result, back, swapped, total, weights, listed, w_gate, w_up, w_down, fetched, send, recv,
):
    fetches = fetch(((far_gate, w_gate), (far_up, w_up), (far_down, w_down)), fetched)
    row = lax.axis_index("row")
    place = around()
    z, y, after, before, beside = place
    yh, x, core = row // 8, lax.rem(row // 2, 4), lax.rem(row, 2)

    def partner(o, sign):
        a, b, d = o // 8, (o // 2) % 4, o % 2
        there = lax.rem(yh + a, 2) * 8 + lax.rem(x + sign * b + 4, 4) * 2 + lax.rem(core + d, 2)
        return (there, z * 2 + lax.rem(y + a, 2))

    partners = [partner(o, 1) for o in range(1, 16)]
    barrier = greet([after, before, beside] + partners)
    offsets = lax.broadcasted_iota(jnp.int32, (16, 1), 0)
    a, b, d = offsets // 8, lax.rem(offsets // 2, 4), lax.rem(offsets, 2)
    expert = (
        lax.rem(yh + a, 2) * 8 + lax.rem(x + b, 4) * 2 + lax.rem(core + d, 2)
    ) * 8 + z
    score = scores[...]
    share_of = score / jnp.sum(score, axis=0, keepdims=True)
    hit = jnp.zeros((16, ROWS), jnp.float32)
    weight = jnp.zeros((16, ROWS), jnp.float32)
    for choice in range(TOP):
        match = routes[choice : choice + 1, :] == expert
        hit = hit + jnp.where(match, 1.0, 0.0)
        weight = weight + jnp.where(match, share_of[choice : choice + 1, :], 0.0)
    earlier = lax.broadcasted_iota(jnp.int32, (ROWS, ROWS), 0) < lax.broadcasted_iota(
        jnp.int32, (ROWS, ROWS), 1
    )
    rank = jnp.dot(
        hit.astype(jnp.bfloat16),
        jnp.where(earlier, 1.0, 0.0).astype(jnp.bfloat16),
        preferred_element_type=jnp.float32,
    )
    rank = jnp.where(hit > 0.0, rank, -1.0).astype(jnp.int32)
    slots = lax.broadcasted_iota(jnp.int32, (CAP, ROWS), 0)
    mine = y * HALF_D
    theirs = HALF_D - mine

    def half(start):
        return pl.ds(pl.multiple_of(start, HALF_D), HALF_D)

    def piece(start, tile):
        return pl.ds(pl.multiple_of(start + tile, TILE), TILE)

    started = []

    def go(src, dst, index, device):
        copy = remote(src, dst, send, recv, index, device)
        copy.start()
        started.append(copy)
        return copy

    def choose(chunks):
        picks = []
        for o in chunks:
            chosen = slots == rank[o : o + 1, :]
            picks.append(jnp.where(chosen, 1.0, 0.0).astype(jnp.bfloat16))
            weights[o * CAP : (o + 1) * CAP, :] = jnp.where(chosen, weight[o : o + 1, :], 0.0).astype(
                jnp.bfloat16
            )
        return jnp.concatenate(picks, axis=0)

    arrivals = {}
    for low in SENDS:
        pick = choose((low, low + 1))
        for tile in range(0, HALF_D if low in SPLIT else D, TILE):
            columns = piece(mine, tile) if low in SPLIT else pl.ds(tile, TILE)
            value = jnp.dot(pick, normed[:, columns], preferred_element_type=jnp.float32)
            value = value.astype(jnp.bfloat16).reshape(2, CAP, TILE)
            if low:
                going[low : low + 2, :, columns] = value
            else:
                coming[0, :, columns] = value[0]
                going[1, :, columns] = value[1]
        if low == SENDS[0]:
            pl.semaphore_wait(barrier, 18)
        for o in (low, low + 1):
            if o in SPLIT:
                arrivals[o] = go(going.at[o, :, half(mine)], coming.at[o, :, half(mine)], o, partner(o, 1))
            elif o:
                arrivals[o] = go(going.at[o], coming.at[o], o, partner(o, 1))
    lists = [go(table, listed.at[o], TABLE_SEMS + o, partner(o, 1)) for o in range(1, 16)]
    shared = {}

    def pass_on(o):
        columns = half(theirs if o >= 8 else mine)
        arrivals[o].wait_recv()
        shared[o] = go(coming.at[o, :, columns], coming.at[o, :, columns], SHARE_SEMS + o, beside)

    returns, swaps = {}, {}

    def work(group):
        for o in range(group, group + 4):
            if o in SPLIT:
                shared[o].wait_recv()
            elif o:
                arrivals[o].wait_recv()
        rows = coming[group : group + 4].reshape(4 * CAP, D)
        gate = jnp.dot(rows, w_gate[...], preferred_element_type=jnp.float32)
        up = jnp.dot(rows, w_up[...], preferred_element_type=jnp.float32)
        inner = (gate / (1.0 + jnp.exp(-gate)) * up).astype(jnp.bfloat16)
        for tile in range(0, D, TILE):
            columns = pl.ds(tile, TILE)
            value = jnp.dot(inner, w_down[:, columns], preferred_element_type=jnp.float32)
            result[group : group + 4, :, columns] = value.astype(jnp.bfloat16).reshape(4, CAP, TILE)
        for o in range(group, group + 4):
            if o in SPLIT:
                columns = half(mine if o >= 8 else theirs)
                swaps[o] = go(result.at[o, :, columns], swapped.at[o], SWAP_SEMS + o, beside)
            elif o:
                returns[o] = go(result.at[o], back.at[o], 16 + o, partner(o, -1))

    def give(o):
        columns = half(theirs if o >= 8 else mine)
        swaps[o].wait_recv()
        result[o, :, columns] = (
            result[o, :, columns].astype(jnp.float32) + swapped[o].astype(jnp.float32)
        ).astype(jnp.bfloat16)
        returns[o] = go(result.at[o, :, columns], back.at[o, :, columns], 16 + o, partner(o, -1))

    for copy in fetches:
        copy.wait()
    for task, chunks in PLAN:
        for o in chunks:
            {"pass": pass_on, "work": work, "give": give}[task](o)
    back[0] = result[0]
    for copy in lists:
        copy.wait_recv()
    known = table[...]
    for o in range(1, 16):
        known = known + listed[o]
    tables[...] = known

    def combine(low, high, columns):
        count = (high - low) * CAP
        return lax.dot_general(
            weights[low * CAP : high * CAP, :],
            back[low:high, :, columns].reshape(count, TILE),
            (((0,), (0,)), ((), ())),
            preferred_element_type=jnp.float32,
        )

    for low, high in WHOLE_RUNS:
        for o in range(max(low, 1), high):
            returns[o].wait_recv()
        for tile in range(0, D, TILE):
            columns = pl.ds(tile, TILE)
            value = combine(low, high, columns)
            total[:, columns] = value if low == 0 else total[:, columns] + value

    def settle(columns, value):
        value = by_block(value.astype(jnp.bfloat16))
        blocks[0, :, :, columns] = value[:, 0]
        blocks[1, :, :, columns] = value[:, 1]

    for tile in range(0, HALF_D, TILE):
        columns = piece(theirs, tile)
        settle(columns, total[:, columns])
    for low, high in SPLIT_RUNS:
        for o in range(low, high):
            returns[o].wait_recv()
        for tile in range(0, HALF_D, TILE):
            columns = piece(mine, tile)
            value = total[:, columns] + combine(low, high, columns)
            if (low, high) == SPLIT_RUNS[-1]:
                settle(columns, value)
            else:
                total[:, columns] = value
    left, right, ring = reduce_blocks(
        place, blocks, y_left, up_left, down_left, up_right, down_right, y_right, send, recv, RING_BASE
    )
    full[z, y, :, LEFT] = (mid[:, :HALF_D].astype(jnp.float32) + left).astype(jnp.bfloat16)
    full[z, y, :, RIGHT] = (mid[:, HALF_D:].astype(jnp.float32) + right).astype(jnp.bfloat16)
    started = started + ring + gather_blocks(place, full, send, recv, RING_BASE + RING_SEMS)
    own = pl.ds(pl.multiple_of((z * 2 + y) * 128, 128), 128)
    share[...] = full[:, :, :, own].reshape(ROWS, 128)
    for copy in started:
        copy.wait_send()


def experts(normed, routes, scores, w_gate, w_up, w_down, mid, table):
    vmem = pl.BlockSpec(memory_space=pltpu.VMEM)
    sems = TABLE_SEMS + 16
    return pl.pallas_call(
        expert_kernel,
        out_shape=(
            jax.ShapeDtypeStruct((8, 2, BLOCK, D), jnp.bfloat16),
            jax.ShapeDtypeStruct((ROWS, 128), jnp.bfloat16),
            jax.ShapeDtypeStruct((8, 128), jnp.int32),
        ),
        in_specs=[vmem] * 3 + [pl.BlockSpec(memory_space=pltpu.HBM)] * 3 + [vmem] * 2,
        out_specs=(vmem, vmem, vmem),
        scratch_shapes=ring_scratch()
        + [
            pltpu.VMEM((16, CAP, D), jnp.bfloat16),
            pltpu.VMEM((16, CAP, D), jnp.bfloat16),
            pltpu.VMEM((16, CAP, D), jnp.bfloat16),
            pltpu.VMEM((16, CAP, D), jnp.bfloat16),
            pltpu.VMEM((16, CAP, HALF_D), jnp.bfloat16),
            pltpu.VMEM((ROWS, D), jnp.float32),
            pltpu.VMEM((16 * CAP, ROWS), jnp.bfloat16),
            pltpu.VMEM((16, 8, 128), jnp.int32),
            pltpu.VMEM((D, 384), jnp.bfloat16),
            pltpu.VMEM((D, 384), jnp.bfloat16),
            pltpu.VMEM((384, D), jnp.bfloat16),
            pltpu.SemaphoreType.DMA((3,)),
            pltpu.SemaphoreType.DMA((sems,)),
            pltpu.SemaphoreType.DMA((sems,)),
        ],
        compiler_params=pltpu.CompilerParams(
            collective_id=1, has_side_effects=True, vmem_limit_bytes=56 << 20
        ),
        name="experts",
    )(normed, routes, scores, w_gate, w_up, w_down, mid, table)


SCALE = HD ** (-0.5)
PACK = 384


def turn(value, cosine, sine):
    return value * cosine + pltpu.roll(value, HD // 2, value.ndim - 1) * sine


def stats_of(top, mass, lane):
    return jnp.where(
        lane == 0, top[0], jnp.where(lane == 1, top[1], jnp.where(lane == 2, mass[0], mass[1]))
    )


def attend_kernel(
    full, gain, far_query, far_keyval, far_cosine, far_sine, segment_column, segment_row, holders, tables,
    far_keys, far_values, new_cache, attention,
    x_in, query, pieces, keys, values, own_query, all_query, slot_query, slots_query,
    parts, parts_in, reply, replies, w_query, w_keyval, cosine, sine, cache_keys, cache_values, fetched, send, recv,
):
    fetches = fetch(
        (
            (far_query, w_query),
            (far_cosine, cosine),
            (far_sine, sine),
            (far_keyval, w_keyval),
            (far_keys, cache_keys),
            (far_values, cache_values),
        ),
        fetched,
    )
    row = lax.axis_index("row")
    col = lax.axis_index("col")
    quarter = lax.rem(col, 4)
    first = col - quarter

    def along_row(o):
        return (lax.rem(row + o, 16), col)

    def along_col(o):
        return (row, lax.rem(col + o, 16))

    barrier = greet([along_row(o) for o in range(1, 16)] + [along_col(o) for o in range(1, 16)])
    started = []

    def go(src, dst, index, device):
        copy = remote(src, dst, send, recv, index, device)
        copy.start()
        started.append(copy)
        return copy

    gains = gain[...].astype(jnp.float32)

    def norm(value):
        value = value.astype(jnp.float32)
        inverse = lax.rsqrt(jnp.mean(value * value, axis=-1, keepdims=True) + EPSILON)
        return (value * inverse * gains).astype(jnp.bfloat16)

    for copy in fetches[:3]:
        copy.wait()
    early = jnp.dot(norm(full[:16, :]), w_query[...], preferred_element_type=jnp.float32)
    early = early.astype(jnp.bfloat16).astype(jnp.float32)
    for head in range(2):
        span = pl.ds(head * HD, HD)
        turned = turn(early[:, head * HD : (head + 1) * HD], cosine[:16, :], sine[:16, :])
        own_query[:, span] = turned.astype(jnp.bfloat16).astype(jnp.float32)[:8]
    all_query[row] = own_query[...]
    pl.semaphore_wait(barrier, 30)
    asks = [go(own_query, all_query.at[row], o, along_row(o)) for o in range(1, 16)]
    for tile in range(0, ROWS, 64):
        x_in[tile : tile + 64, :] = norm(full[tile : tile + 64, :])
    for copy in fetches[3:]:
        copy.wait()
    keyval = jnp.dot(x_in[...], w_keyval[...], preferred_element_type=jnp.float32).astype(jnp.bfloat16)
    pieces[quarter] = jnp.concatenate([keyval[: ROWS // 2], keyval[ROWS // 2 :]], axis=1)
    shares = [
        go(pieces.at[quarter], pieces.at[quarter], 16 + o, (row, first + lax.rem(quarter + o, 4)))
        for o in range(1, 4)
    ]
    for copy in asks:
        copy.wait_recv()
    held = (
        tables[0:1, :] == row * 8 + lax.broadcasted_iota(jnp.int32, (8, 128), 0)
    )
    length = jnp.sum(jnp.where(held, tables[1:2, :], 0), axis=1, keepdims=True)
    slot_query[...] = jnp.dot(
        jnp.where(held, 1.0, 0.0).astype(jnp.bfloat16),
        all_query[...].reshape(128, 2 * HD).astype(jnp.bfloat16),
        preferred_element_type=jnp.float32,
    )
    slots_query[col] = slot_query[...]
    tells = [go(slot_query, slots_query.at[col], 20 + o, along_col(o)) for o in range(1, 16)]
    for head in range(2):
        span = pl.ds(head * HD, HD)
        value = jnp.dot(x_in[...], w_query[:, span], preferred_element_type=jnp.float32)
        value = value.astype(jnp.bfloat16).astype(jnp.float32)
        query[:, span] = turn(value, cosine[...], sine[...]).astype(jnp.bfloat16)
    for copy in tells:
        copy.wait_recv()
    group = lax.rem(lax.broadcasted_iota(jnp.int32, (32, 4 * HD), 0), 16) // 4
    matched = group == lax.broadcasted_iota(jnp.int32, (32, 4 * HD), 1) // HD
    spot = col * 64 + lax.broadcasted_iota(jnp.int32, (32, 64), 1)
    lane = lax.broadcasted_iota(jnp.int32, (16, HD), 1)
    for slot in range(8):
        asked = slots_query[:, slot, :]
        asked = jnp.concatenate([asked[:, :HD], asked[:, HD:]], axis=0)
        asked = jnp.where(matched, jnp.concatenate([asked] * 4, axis=1), 0.0).astype(jnp.bfloat16)
        scores = SCALE * lax.dot_general(
            asked, cache_keys[slot], (((1,), (1,)), ((), ())), preferred_element_type=jnp.float32
        )
        valid = spot < length[slot : slot + 1, :]
        scores = jnp.where(valid, scores, NEGATIVE)
        top = jnp.max(scores, axis=1, keepdims=True)
        grown = jnp.where(valid, jnp.exp(scores - top), 0.0)
        mass = jnp.sum(grown, axis=1, keepdims=True)
        blend = jnp.dot(grown.astype(jnp.bfloat16), cache_values[slot], preferred_element_type=jnp.float32)
        blend = jnp.where(matched, blend, 0.0)
        blend = blend[:, :HD] + blend[:, HD : 2 * HD] + blend[:, 2 * HD : 3 * HD] + blend[:, 3 * HD :]
        parts[:, slot, :HD] = blend[:16]
        parts[:, slot, HD : 2 * HD] = blend[16:]
        parts[:, slot, 2 * HD :] = stats_of((top[:16], top[16:]), (mass[:16], mass[16:]), lane)
    parts_in[0] = parts[col]
    sums = [
        go(parts.at[lax.rem(col + o, 16)], parts_in.at[o], 36 + o, along_col(o)) for o in range(1, 16)
    ]
    for copy in shares:
        copy.wait_recv()

    def piece(index):
        value = pieces[index]
        return jnp.concatenate([value[:, : HD // 2], value[:, HD // 2 :]], axis=0)

    quarters = [piece(index) for index in range(4)]
    key = jnp.concatenate(quarters[:2], axis=1).astype(jnp.float32)
    keys[...] = turn(key, cosine[...], sine[...]).astype(jnp.bfloat16)
    values[...] = jnp.concatenate(quarters[2:], axis=1)
    new_cache[...] = jnp.where(
        quarter == 0,
        keys[:, : HD // 2],
        jnp.where(
            quarter == 1,
            keys[:, HD // 2 :],
            jnp.where(quarter == 2, values[:, : HD // 2], values[:, HD // 2 :]),
        ),
    )

    def prompt(head):
        span = pl.ds(head * HD, HD)
        for tile in range(0, ROWS, 128):
            reach = tile + 128
            scores = SCALE * lax.dot_general(
                query[tile:reach, span], keys[:reach, :], (((1,), (1,)), ((), ())),
                preferred_element_type=jnp.float32,
            )
            allowed = (segment_column[tile:reach, :] == segment_row[:, :reach]) & (
                lax.broadcasted_iota(jnp.int32, (128, reach), 1)
                <= lax.broadcasted_iota(jnp.int32, (128, reach), 0) + tile
            )
            scores = jnp.where(allowed, scores, NEGATIVE)
            grown = jnp.exp(scores - jnp.max(scores, axis=1, keepdims=True))
            chance = (grown / jnp.sum(grown, axis=1, keepdims=True)).astype(jnp.bfloat16)
            attention[tile:reach, span] = jnp.dot(
                chance, values[:reach, :], preferred_element_type=jnp.float32
            ).astype(jnp.bfloat16)

    prompt(0)
    for copy in sums:
        copy.wait_recv()
    tops, masses = [], []
    for head in range(2):
        top = parts_in[:, :, 2 * HD + head : 2 * HD + head + 1]
        mass = parts_in[:, :, 2 * HD + 2 + head : 2 * HD + 3 + head]
        highest = jnp.max(top, axis=0)
        factor = jnp.exp(top - highest[None])
        span = pl.ds(head * HD, HD)
        reply[:, span] = jnp.sum(parts_in[:, :, span] * factor, axis=0)
        tops.append(highest)
        masses.append(jnp.sum(mass * factor, axis=0))
    reply[:, 2 * HD :] = stats_of(tops, masses, lane[:8])
    replies[row] = reply[...]
    backs = [go(reply, replies.at[row], 52 + o, along_row(o)) for o in range(1, 16)]
    prompt(1)
    for copy in backs:
        copy.wait_recv()
    mine = jnp.where(holders[...] == lax.broadcasted_iota(jnp.int32, (8, 128), 1), 1.0, 0.0)
    got = jnp.dot(
        mine,
        replies[...].reshape(128, PACK),
        preferred_element_type=jnp.float32,
        precision=lax.Precision.HIGHEST,
    )
    own_key = keys[:16, :].astype(jnp.float32)[:8]
    own_value = values[:16, :].astype(jnp.float32)[:8]
    for head in range(2):
        span = pl.ds(head * HD, HD)
        own = SCALE * jnp.sum(own_query[:, span] * own_key, axis=1, keepdims=True)
        top = got[:, 2 * HD + head : 2 * HD + head + 1]
        mass = got[:, 2 * HD + 2 + head : 2 * HD + 3 + head]
        highest = jnp.maximum(top, own)
        theirs = jnp.exp(top - highest)
        ours = jnp.exp(own - highest)
        result = (got[:, head * HD : (head + 1) * HD] * theirs + own_value * ours) / (mass * theirs + ours)
        result = jnp.concatenate([result, result], axis=0)
        decoded = lax.broadcasted_iota(jnp.int32, (16, HD), 0) < 8
        attention[:16, span] = jnp.where(
            decoded, result, attention[:16, span].astype(jnp.float32)
        ).astype(jnp.bfloat16)
    for copy in started:
        copy.wait_send()


def attend(full, gain, w_query, w_keyval, cosine, sine, segments, holders, tables, cache_keys, cache_values):
    vmem = pl.BlockSpec(memory_space=pltpu.VMEM)
    far = pl.BlockSpec(memory_space=pltpu.HBM)
    f32, bf16 = jnp.float32, jnp.bfloat16
    return pl.pallas_call(
        attend_kernel,
        out_shape=(
            jax.ShapeDtypeStruct((ROWS, 64), bf16),
            jax.ShapeDtypeStruct((ROWS, 2 * HD), bf16),
        ),
        in_specs=[vmem] * 2 + [far] * 4 + [vmem] * 4 + [far] * 2,
        out_specs=(vmem, vmem),
        scratch_shapes=[
            pltpu.VMEM((ROWS, D), bf16),
            pltpu.VMEM((ROWS, 2 * HD), bf16),
            pltpu.VMEM((4, ROWS // 2, HD), bf16),
            pltpu.VMEM((ROWS, HD), bf16),
            pltpu.VMEM((ROWS, HD), bf16),
            pltpu.VMEM((8, 2 * HD), f32),
            pltpu.VMEM((16, 8, 2 * HD), f32),
            pltpu.VMEM((8, 2 * HD), f32),
            pltpu.VMEM((16, 8, 2 * HD), f32),
            pltpu.VMEM((16, 8, PACK), f32),
            pltpu.VMEM((16, 8, PACK), f32),
            pltpu.VMEM((8, PACK), f32),
            pltpu.VMEM((16, 8, PACK), f32),
            pltpu.VMEM((D, 2 * HD), bf16),
            pltpu.VMEM((D, 64), bf16),
            pltpu.VMEM((ROWS, HD), f32),
            pltpu.VMEM((ROWS, HD), f32),
            pltpu.VMEM((8, 64, 4 * HD), bf16),
            pltpu.VMEM((8, 64, 4 * HD), bf16),
            pltpu.SemaphoreType.DMA((6,)),
            pltpu.SemaphoreType.DMA((68,)),
            pltpu.SemaphoreType.DMA((68,)),
        ],
        compiler_params=pltpu.CompilerParams(
            collective_id=2, has_side_effects=True, vmem_limit_bytes=48 << 20
        ),
        name="attend",
    )(
        full, gain.reshape(1, D), w_query, w_keyval, cosine, sine,
        segments.reshape(ROWS, 1), segments.reshape(1, ROWS), holders.reshape(8, 1), tables,
        cache_keys, cache_values,
    )


def shards(
    attn_context,
    residual,
    w_out,
    gain_post,
    gain_input,
    routes,
    router_scores,
    w_gate,
    w_up,
    w_down,
    w_query,
    w_keyval,
    segment_ids,
    cache_lengths,
    holders,
    cache_keys,
    cache_values,
):
    row = lax.axis_index("row")
    segment = segment_ids[0]
    earlier = jnp.sum((segment[None, :] < segment[:, None]).astype(jnp.int32), axis=1)
    position = jnp.concatenate([cache_lengths, jnp.arange(segment.shape[0], dtype=jnp.int32) - earlier])
    indices = jnp.arange(HD // 2).astype(jnp.float32)
    angles = position.astype(jnp.float32)[:, None] * (ROPE_THETA ** (-2.0 * indices / HD))[None, :]
    cosine, sine = jnp.cos(angles), jnp.sin(angles)
    cosine = jnp.concatenate([cosine, cosine], axis=1)
    sine = jnp.concatenate([-sine, sine], axis=1)
    segments = jnp.concatenate([jnp.full((8,), -1, jnp.int32), segment])
    table = jnp.stack([holders, cache_lengths])
    table = jnp.pad(table, ((0, 6), (0, 0)))
    table = jnp.where(
        jnp.arange(128, dtype=jnp.int32)[None, :] // 8 == row, jnp.tile(table, (1, 16)), 0
    )
    normed, mid = out_project(attn_context, w_out, residual, gain_post)
    full, hidden_out, tables = experts(
        normed.reshape(ROWS, D), routes.T, router_scores.T, w_gate[0], w_up[0], w_down[0], mid, table
    )
    new_cache, attention_out = attend(
        full.reshape(ROWS, D), gain_input, w_query, w_keyval, cosine, sine, segments, holders, tables,
        cache_keys, cache_values,
    )
    return (hidden_out, new_cache, attention_out)


def solution(mesh):
    return jax.shard_map(
        shards,
        mesh=mesh,
        in_specs=(
            P("row", "col"),
            P("row", "col"),
            P("col", None),
            P(),
            P(),
            P("row", None),
            P("row", None),
            P(("row", "col"), None, None),
            P(("row", "col"), None, None),
            P(("row", "col"), None, None),
            P(None, "col"),
            P(None, "col"),
            P("row", None),
            P("row"),
            P("row"),
            P("row", "col", None),
            P("row", "col", None),
        ),
        out_specs=(P("row", "col"), P("row", "col"), P("row", "col")),
        check_vma=False,
    )
```

```python
import functools

import jax
import jax.numpy as jnp
from jax import lax
from jax.experimental import pallas as pl
from jax.experimental.pallas import tpu as pltpu
from jax.sharding import PartitionSpec as P

TOP = 8
QH = 32
KVH = 4
HD = 128
EPSILON = 1e-06
ROPE_THETA = 1000000.0
NEGATIVE = -1e30
MESH = pl.DeviceIdType.MESH

D = 2048
HALF_D = 1024
LEFT = pl.ds(0, HALF_D)
RIGHT = pl.ds(HALF_D, HALF_D)
ROWS = 512
BLOCK = 32
CAP = 64
RING_SEMS = 23
TILE = 512


def remote(src, dst, send, recv, index, device):
    return pltpu.make_async_remote_copy(
        src_ref=src,
        dst_ref=dst,
        send_sem=send.at[index],
        recv_sem=recv.at[index],
        device_id=device,
        device_id_type=MESH,
    )


def around():
    row = lax.axis_index("row")
    col = lax.axis_index("col")
    z = col // 2
    y = lax.rem(col, 2)
    after = (row, lax.rem(z + 1, 8) * 2 + y)
    before = (row, lax.rem(z + 7, 8) * 2 + y)
    beside = (row, z * 2 + 1 - y)
    return z, y, after, before, beside


def reduce_blocks(place, blocks, y_left, up_left, down_left, up_right, down_right, y_right, send, recv, base):
    z, y, after, before, beside = place
    other = 1 - y
    started = []

    def go(src, dst, index, device):
        copy = remote(src, dst, send, recv, base + index, device)
        copy.start()
        started.append(copy)
        return copy

    def at(offset):
        return lax.rem(z + offset + 8, 8)

    crossing = {}
    for index, offset in enumerate((4, -3, 3, -2, 2, -1, 1, 0)):
        t = at(offset)
        crossing[offset] = go(blocks.at[other, t, :, LEFT], y_left.at[t], index, beside)
    up_l, down_l, up_r, down_r = [], [], [], []
    for step in range(4):
        if step < 3:
            t = at(3 - step)
            if step:
                up_r[-1].wait_recv()
                blocks[:, t, :, RIGHT] = (
                    blocks[:, t, :, RIGHT].astype(jnp.float32) + up_right[step - 1].astype(jnp.float32)
                ).astype(jnp.bfloat16)
            up_r.append(go(blocks.at[:, t, :, RIGHT], up_right.at[step], 8 + step, after))
        t = at(step - 4)
        if step:
            down_r[-1].wait_recv()
            blocks[:, t, :, RIGHT] = (
                blocks[:, t, :, RIGHT].astype(jnp.float32) + down_right[step - 1].astype(jnp.float32)
            ).astype(jnp.bfloat16)
        down_r.append(go(blocks.at[:, t, :, RIGHT], down_right.at[step], 11 + step, before))
        t = at(4 - step)
        crossing[4 - step].wait_recv()
        value = blocks[y, t, :, LEFT].astype(jnp.float32) + y_left[t].astype(jnp.float32)
        if step:
            up_l[-1].wait_recv()
            value = value + up_left[step - 1].astype(jnp.float32)
        blocks[y, t, :, LEFT] = value.astype(jnp.bfloat16)
        up_l.append(go(blocks.at[y, t, :, LEFT], up_left.at[step], 15 + step, after))
        if step < 3:
            t = at(step - 3)
            crossing[step - 3].wait_recv()
            value = blocks[y, t, :, LEFT].astype(jnp.float32) + y_left[t].astype(jnp.float32)
            if step:
                down_l[-1].wait_recv()
                value = value + down_left[step - 1].astype(jnp.float32)
            blocks[y, t, :, LEFT] = value.astype(jnp.bfloat16)
            down_l.append(go(blocks.at[y, t, :, LEFT], down_left.at[step], 19 + step, before))
    up_r[-1].wait_recv()
    down_r[-1].wait_recv()
    blocks[other, z, :, RIGHT] = (
        blocks[other, z, :, RIGHT].astype(jnp.float32)
        + up_right[2, other].astype(jnp.float32)
        + down_right[3, other].astype(jnp.float32)
    ).astype(jnp.bfloat16)
    last = go(blocks.at[other, z, :, RIGHT], y_right, 22, beside)
    right = (
        blocks[y, z, :, RIGHT].astype(jnp.float32)
        + up_right[2, y].astype(jnp.float32)
        + down_right[3, y].astype(jnp.float32)
    )
    crossing[0].wait_recv()
    up_l[-1].wait_recv()
    down_l[-1].wait_recv()
    left = (
        blocks[y, z, :, LEFT].astype(jnp.float32)
        + y_left[z].astype(jnp.float32)
        + up_left[3].astype(jnp.float32)
        + down_left[2].astype(jnp.float32)
    )
    last.wait_recv()
    right = right + y_right[...].astype(jnp.float32)
    return left, right, started


def gather_blocks(place, full, send, recv, base):
    z, y, after, before, beside = place
    started = []

    def go(view, index, device):
        copy = remote(view, view, send, recv, base + index, device)
        copy.start()
        started.append(copy)
        return copy

    def at(offset):
        return lax.rem(z + offset + 8, 8)

    first = go(full.at[z, y, :, RIGHT], 0, beside)
    crossing = []
    up_l, down_l, up_r, down_r = [], [], [], []

    def cross(t):
        crossing.append(go(full.at[t, y, :, LEFT], 1 + len(crossing), beside))

    for step in range(4):
        if step:
            up_l[-1].wait_recv()
        up_l.append(go(full.at[at(-step), y, :, LEFT], 9 + step, after))
        if step < 3:
            if step:
                down_l[-1].wait_recv()
            down_l.append(go(full.at[at(step), y, :, LEFT], 13 + step, before))
        if step == 0:
            first.wait_recv()
        if step < 3:
            if step:
                up_r[-1].wait_recv()
            up_r.append(go(full.at[at(-step), :, :, RIGHT], 16 + step, after))
        if step:
            down_r[-1].wait_recv()
        down_r.append(go(full.at[at(step), :, :, RIGHT], 19 + step, before))
        cross(at(-step))
        if 0 < step < 3:
            cross(at(step))
    down_l[-1].wait_recv()
    cross(at(3))
    up_l[-1].wait_recv()
    cross(at(-4))
    up_r[-1].wait_recv()
    down_r[-1].wait_recv()
    for copy in crossing:
        copy.wait_recv()
    return started


def ring_scratch():
    return [
        pltpu.VMEM((2, 8, BLOCK, D), jnp.bfloat16),
        pltpu.VMEM((8, BLOCK, HALF_D), jnp.bfloat16),
        pltpu.VMEM((4, BLOCK, HALF_D), jnp.bfloat16),
        pltpu.VMEM((3, BLOCK, HALF_D), jnp.bfloat16),
        pltpu.VMEM((3, 2, BLOCK, HALF_D), jnp.bfloat16),
        pltpu.VMEM((4, 2, BLOCK, HALF_D), jnp.bfloat16),
        pltpu.VMEM((BLOCK, HALF_D), jnp.bfloat16),
    ]


def greet(devices):
    barrier = pltpu.get_barrier_semaphore()
    for device in devices:
        pl.semaphore_signal(barrier, inc=1, device_id=device, device_id_type=MESH)
    return barrier


def by_block(value):
    return value.reshape(8, 2, BLOCK, value.shape[-1])


def fetch(pairs, sems):
    copies = [pltpu.make_async_copy(far, near, sems.at[index]) for index, (far, near) in enumerate(pairs)]
    for copy in copies:
        copy.start()
    return copies


def project(context, w_out, residual, gain, normed, mid, blocks, buffers, send, recv, wait_for_all):
    place = around()
    z, y = place[:2]
    for tile in range(0, D, TILE):
        columns = pl.ds(tile, TILE)
        value = by_block(
            jnp.dot(context[...], w_out[:, columns], preferred_element_type=jnp.float32).astype(jnp.bfloat16)
        )
        blocks[0, :, :, columns] = value[:, 0]
        blocks[1, :, :, columns] = value[:, 1]
    own = pl.ds(pl.multiple_of((z * 2 + y) * 128, 128), 128)
    value = jnp.dot(context[...], w_out[:, own], preferred_element_type=jnp.float32)
    value = by_block((value + residual[...].astype(jnp.float32)).astype(jnp.bfloat16))
    blocks[0, :, :, own] = value[:, 0]
    blocks[1, :, :, own] = value[:, 1]
    wait_for_all()
    left, right, started = reduce_blocks(place, blocks, *buffers, send, recv, 0)
    left = left.astype(jnp.bfloat16)
    right = right.astype(jnp.bfloat16)
    mid[:, :HALF_D] = left
    mid[:, HALF_D:] = right
    left = left.astype(jnp.float32)
    right = right.astype(jnp.float32)
    mean = (
        jnp.sum(left * left, axis=-1, keepdims=True) + jnp.sum(right * right, axis=-1, keepdims=True)
    ) * (1.0 / D)
    inverse = lax.rsqrt(mean + EPSILON)
    gains = gain[...].astype(jnp.float32)
    normed[z, y, :, LEFT] = (left * inverse * gains[:, :HALF_D]).astype(jnp.bfloat16)
    normed[z, y, :, RIGHT] = (right * inverse * gains[:, HALF_D:]).astype(jnp.bfloat16)
    return started + gather_blocks(place, normed, send, recv, RING_SEMS)


SPLIT = (4, 5, 10, 11, 12, 13, 14, 15)
SENDS = (12, 14, 2, 10, 4, 6, 8, 0)
PLAN = (
    ('pass', (12, 13, 14, 15)),
    ('work', (0,)),
    ('pass', (10, 11)),
    ('work', (12,)),
    ('pass', (4, 5)),
    ('work', (8,)),
    ('give', (12, 13, 14, 15)),
    ('work', (4,)),
    ('give', (10, 11, 4, 5)),
)
WHOLE_RUNS = ((0, 4), (6, 10))
SPLIT_RUNS = ((10, 12), (12, 16), (4, 6))
SHARE_SEMS = 32
SWAP_SEMS = 48
RING_BASE = 64
TABLE_SEMS = RING_BASE + 2 * RING_SEMS


def partner(o, sign):
    row = lax.axis_index("row")
    col = lax.axis_index("col")
    z, y = col // 2, lax.rem(col, 2)
    yh, x, core = row // 8, lax.rem(row // 2, 4), lax.rem(row, 2)
    a, b, d = o // 8, (o // 2) % 4, o % 2
    there = lax.rem(yh + a, 2) * 8 + lax.rem(x + sign * b + 4, 4) * 2 + lax.rem(core + d, 2)
    return (there, z * 2 + lax.rem(y + a, 2))


def apply_experts(
    normed, routes, scores, w_gate, w_up, w_down, fetches, mid, table, full, share, tables,
    blocks, buffers, going, coming, result, back, swapped, total, weights, listed, send, recv,
):
    row = lax.axis_index("row")
    place = around()
    z, y, after, before, beside = place
    yh, x, core = row // 8, lax.rem(row // 2, 4), lax.rem(row, 2)

    offsets = lax.broadcasted_iota(jnp.int32, (16, 1), 0)
    a, b, d = offsets // 8, lax.rem(offsets // 2, 4), lax.rem(offsets, 2)
    expert = (
        lax.rem(yh + a, 2) * 8 + lax.rem(x + b, 4) * 2 + lax.rem(core + d, 2)
    ) * 8 + z
    score = scores[...]
    share_of = score / jnp.sum(score, axis=0, keepdims=True)
    hit = jnp.zeros((16, ROWS), jnp.float32)
    weight = jnp.zeros((16, ROWS), jnp.float32)
    for choice in range(TOP):
        match = routes[choice : choice + 1, :] == expert
        hit = hit + jnp.where(match, 1.0, 0.0)
        weight = weight + jnp.where(match, share_of[choice : choice + 1, :], 0.0)
    earlier = lax.broadcasted_iota(jnp.int32, (ROWS, ROWS), 0) < lax.broadcasted_iota(
        jnp.int32, (ROWS, ROWS), 1
    )
    rank = jnp.dot(
        hit.astype(jnp.bfloat16),
        jnp.where(earlier, 1.0, 0.0).astype(jnp.bfloat16),
        preferred_element_type=jnp.float32,
    )
    rank = jnp.where(hit > 0.0, rank, -1.0).astype(jnp.int32)
    slots = lax.broadcasted_iota(jnp.int32, (CAP, ROWS), 0)
    mine = y * HALF_D
    theirs = HALF_D - mine

    def half(start):
        return pl.ds(pl.multiple_of(start, HALF_D), HALF_D)

    def piece(start, tile):
        return pl.ds(pl.multiple_of(start + tile, TILE), TILE)

    started = []

    def go(src, dst, index, device):
        copy = remote(src, dst, send, recv, index, device)
        copy.start()
        started.append(copy)
        return copy

    def choose(chunks):
        picks = []
        for o in chunks:
            chosen = slots == rank[o : o + 1, :]
            picks.append(jnp.where(chosen, 1.0, 0.0).astype(jnp.bfloat16))
            weights[o * CAP : (o + 1) * CAP, :] = jnp.where(chosen, weight[o : o + 1, :], 0.0).astype(
                jnp.bfloat16
            )
        return jnp.concatenate(picks, axis=0)

    arrivals = {}
    for low in SENDS:
        pick = choose((low, low + 1))
        for tile in range(0, HALF_D if low in SPLIT else D, TILE):
            columns = piece(mine, tile) if low in SPLIT else pl.ds(tile, TILE)
            rows = normed[:, :, :, columns].reshape(ROWS, TILE)
            value = jnp.dot(pick, rows, preferred_element_type=jnp.float32)
            value = value.astype(jnp.bfloat16).reshape(2, CAP, TILE)
            if low:
                going[low : low + 2, :, columns] = value
            else:
                coming[0, :, columns] = value[0]
                going[1, :, columns] = value[1]
        for o in (low, low + 1):
            if o in SPLIT:
                arrivals[o] = go(going.at[o, :, half(mine)], coming.at[o, :, half(mine)], o, partner(o, 1))
            elif o:
                arrivals[o] = go(going.at[o], coming.at[o], o, partner(o, 1))
    lists = [go(table, listed.at[o], TABLE_SEMS + o, partner(o, 1)) for o in range(1, 16)]
    shared = {}

    def pass_on(o):
        columns = half(theirs if o >= 8 else mine)
        arrivals[o].wait_recv()
        shared[o] = go(coming.at[o, :, columns], coming.at[o, :, columns], SHARE_SEMS + o, beside)

    returns, swaps = {}, {}

    def work(group):
        for o in range(group, group + 4):
            if o in SPLIT:
                shared[o].wait_recv()
            elif o:
                arrivals[o].wait_recv()
        rows = coming[group : group + 4].reshape(4 * CAP, D)
        gate = jnp.dot(rows, w_gate[...], preferred_element_type=jnp.float32)
        up = jnp.dot(rows, w_up[...], preferred_element_type=jnp.float32)
        inner = (gate / (1.0 + jnp.exp(-gate)) * up).astype(jnp.bfloat16)
        for tile in range(0, D, TILE):
            columns = pl.ds(tile, TILE)
            value = jnp.dot(inner, w_down[:, columns], preferred_element_type=jnp.float32)
            result[group : group + 4, :, columns] = value.astype(jnp.bfloat16).reshape(4, CAP, TILE)
        for o in range(group, group + 4):
            if o in SPLIT:
                columns = half(mine if o >= 8 else theirs)
                swaps[o] = go(result.at[o, :, columns], swapped.at[o], SWAP_SEMS + o, beside)
            elif o:
                returns[o] = go(result.at[o], back.at[o], 16 + o, partner(o, -1))

    def give(o):
        columns = half(theirs if o >= 8 else mine)
        swaps[o].wait_recv()
        result[o, :, columns] = (
            result[o, :, columns].astype(jnp.float32) + swapped[o].astype(jnp.float32)
        ).astype(jnp.bfloat16)
        returns[o] = go(result.at[o, :, columns], back.at[o, :, columns], 16 + o, partner(o, -1))

    for copy in fetches:
        copy.wait()
    for task, chunks in PLAN:
        for o in chunks:
            {"pass": pass_on, "work": work, "give": give}[task](o)
    back[0] = result[0]
    for copy in lists:
        copy.wait_recv()
    known = table[...]
    for o in range(1, 16):
        known = known + listed[o]
    tables[...] = known

    def combine(low, high, columns):
        count = (high - low) * CAP
        return lax.dot_general(
            weights[low * CAP : high * CAP, :],
            back[low:high, :, columns].reshape(count, TILE),
            (((0,), (0,)), ((), ())),
            preferred_element_type=jnp.float32,
        )

    for low, high in WHOLE_RUNS:
        for o in range(max(low, 1), high):
            returns[o].wait_recv()
        for tile in range(0, D, TILE):
            columns = pl.ds(tile, TILE)
            value = combine(low, high, columns)
            total[:, columns] = value if low == 0 else total[:, columns] + value

    def settle(columns, value):
        value = by_block(value.astype(jnp.bfloat16))
        blocks[0, :, :, columns] = value[:, 0]
        blocks[1, :, :, columns] = value[:, 1]

    for tile in range(0, HALF_D, TILE):
        columns = piece(theirs, tile)
        settle(columns, total[:, columns])
    for low, high in SPLIT_RUNS:
        for o in range(low, high):
            returns[o].wait_recv()
        for tile in range(0, HALF_D, TILE):
            columns = piece(mine, tile)
            value = total[:, columns] + combine(low, high, columns)
            if (low, high) == SPLIT_RUNS[-1]:
                settle(columns, value)
            else:
                total[:, columns] = value
    left, right, ring = reduce_blocks(
        place, blocks, *buffers, send, recv, RING_BASE
    )
    full[z, y, :, LEFT] = (mid[:, :HALF_D].astype(jnp.float32) + left).astype(jnp.bfloat16)
    full[z, y, :, RIGHT] = (mid[:, HALF_D:].astype(jnp.float32) + right).astype(jnp.bfloat16)
    started = started + ring + gather_blocks(place, full, send, recv, RING_BASE + RING_SEMS)
    own = pl.ds(pl.multiple_of((z * 2 + y) * 128, 128), 128)
    share[...] = full[:, :, :, own].reshape(ROWS, 128)
    return started


SCALE = HD ** (-0.5)
PACK = 384


def turn(value, cosine, sine):
    return value * cosine + pltpu.roll(value, HD // 2, value.ndim - 1) * sine


def stats_of(top, mass, lane):
    return jnp.where(
        lane == 0, top[0], jnp.where(lane == 1, top[1], jnp.where(lane == 2, mass[0], mass[1]))
    )


def along_row(o):
    return (lax.rem(lax.axis_index("row") + o, 16), lax.axis_index("col"))


def along_col(o):
    return (lax.axis_index("row"), lax.rem(lax.axis_index("col") + o, 16))


def attend(
    full, gain, w_query, w_keyval, cosine, sine, fetches, segment_column, segment_row, holders, tables,
    cache_keys, cache_values, new_cache, attention,
    x_in, query, pieces, keys, values, own_query, all_query, slot_query, slots_query,
    parts, parts_in, reply, replies, send, recv,
):
    row = lax.axis_index("row")
    col = lax.axis_index("col")
    quarter = lax.rem(col, 4)
    first = col - quarter

    started = []

    def go(src, dst, index, device):
        copy = remote(src, dst, send, recv, index, device)
        copy.start()
        started.append(copy)
        return copy

    gains = gain[...].astype(jnp.float32)

    def norm(value):
        value = value.astype(jnp.float32)
        inverse = lax.rsqrt(jnp.mean(value * value, axis=-1, keepdims=True) + EPSILON)
        return (value * inverse * gains).astype(jnp.bfloat16)

    for copy in fetches:
        copy.wait()
    early = jnp.dot(norm(full[0, 0, :16, :]), w_query[...], preferred_element_type=jnp.float32)
    early = early.astype(jnp.bfloat16).astype(jnp.float32)
    for head in range(2):
        span = pl.ds(head * HD, HD)
        turned = turn(early[:, head * HD : (head + 1) * HD], cosine[:16, :], sine[:16, :])
        own_query[:, span] = turned.astype(jnp.bfloat16).astype(jnp.float32)[:8]
    all_query[row] = own_query[...]
    asks = [go(own_query, all_query.at[row], o, along_row(o)) for o in range(1, 16)]
    for tile in range(0, ROWS, 64):
        x_in[tile : tile + 64, :] = norm(full[tile // 64].reshape(64, D))
    keyval = jnp.dot(x_in[...], w_keyval[...], preferred_element_type=jnp.float32).astype(jnp.bfloat16)
    pieces[quarter] = jnp.concatenate([keyval[: ROWS // 2], keyval[ROWS // 2 :]], axis=1)
    shares = [
        go(pieces.at[quarter], pieces.at[quarter], 16 + o, (row, first + lax.rem(quarter + o, 4)))
        for o in range(1, 4)
    ]
    for copy in asks:
        copy.wait_recv()
    held = (
        tables[0:1, :] == row * 8 + lax.broadcasted_iota(jnp.int32, (8, 128), 0)
    )
    length = jnp.sum(jnp.where(held, tables[1:2, :], 0), axis=1, keepdims=True)
    slot_query[...] = jnp.dot(
        jnp.where(held, 1.0, 0.0).astype(jnp.bfloat16),
        all_query[...].reshape(128, 2 * HD).astype(jnp.bfloat16),
        preferred_element_type=jnp.float32,
    )
    slots_query[col] = slot_query[...]
    tells = [go(slot_query, slots_query.at[col], 20 + o, along_col(o)) for o in range(1, 16)]
    for head in range(2):
        span = pl.ds(head * HD, HD)
        value = jnp.dot(x_in[...], w_query[:, span], preferred_element_type=jnp.float32)
        value = value.astype(jnp.bfloat16).astype(jnp.float32)
        query[:, span] = turn(value, cosine[...], sine[...]).astype(jnp.bfloat16)
    for copy in tells:
        copy.wait_recv()
    group = lax.rem(lax.broadcasted_iota(jnp.int32, (32, 4 * HD), 0), 16) // 4
    matched = group == lax.broadcasted_iota(jnp.int32, (32, 4 * HD), 1) // HD
    spot = col * 64 + lax.broadcasted_iota(jnp.int32, (32, 64), 1)
    lane = lax.broadcasted_iota(jnp.int32, (16, HD), 1)
    for slot in range(8):
        asked = slots_query[:, slot, :]
        asked = jnp.concatenate([asked[:, :HD], asked[:, HD:]], axis=0)
        asked = jnp.where(matched, jnp.concatenate([asked] * 4, axis=1), 0.0).astype(jnp.bfloat16)
        scores = SCALE * lax.dot_general(
            asked, cache_keys[slot], (((1,), (1,)), ((), ())), preferred_element_type=jnp.float32
        )
        valid = spot < length[slot : slot + 1, :]
        scores = jnp.where(valid, scores, NEGATIVE)
        top = jnp.max(scores, axis=1, keepdims=True)
        grown = jnp.where(valid, jnp.exp(scores - top), 0.0)
        mass = jnp.sum(grown, axis=1, keepdims=True)
        blend = jnp.dot(grown.astype(jnp.bfloat16), cache_values[slot], preferred_element_type=jnp.float32)
        blend = jnp.where(matched, blend, 0.0)
        blend = blend[:, :HD] + blend[:, HD : 2 * HD] + blend[:, 2 * HD : 3 * HD] + blend[:, 3 * HD :]
        parts[:, slot, :HD] = blend[:16]
        parts[:, slot, HD : 2 * HD] = blend[16:]
        parts[:, slot, 2 * HD :] = stats_of((top[:16], top[16:]), (mass[:16], mass[16:]), lane)
    parts_in[0] = parts[col]
    sums = [
        go(parts.at[lax.rem(col + o, 16)], parts_in.at[o], 36 + o, along_col(o)) for o in range(1, 16)
    ]
    for copy in shares:
        copy.wait_recv()

    def piece(index):
        value = pieces[index]
        return jnp.concatenate([value[:, : HD // 2], value[:, HD // 2 :]], axis=0)

    quarters = [piece(index) for index in range(4)]
    key = jnp.concatenate(quarters[:2], axis=1).astype(jnp.float32)
    keys[...] = turn(key, cosine[...], sine[...]).astype(jnp.bfloat16)
    values[...] = jnp.concatenate(quarters[2:], axis=1)
    new_cache[...] = jnp.where(
        quarter == 0,
        keys[:, : HD // 2],
        jnp.where(
            quarter == 1,
            keys[:, HD // 2 :],
            jnp.where(quarter == 2, values[:, : HD // 2], values[:, HD // 2 :]),
        ),
    )

    def prompt(head):
        span = pl.ds(head * HD, HD)
        for tile in range(0, ROWS, 128):
            reach = tile + 128
            scores = SCALE * lax.dot_general(
                query[tile:reach, span], keys[:reach, :], (((1,), (1,)), ((), ())),
                preferred_element_type=jnp.float32,
            )
            allowed = (segment_column[tile:reach, :] == segment_row[:, :reach]) & (
                lax.broadcasted_iota(jnp.int32, (128, reach), 1)
                <= lax.broadcasted_iota(jnp.int32, (128, reach), 0) + tile
            )
            scores = jnp.where(allowed, scores, NEGATIVE)
            grown = jnp.exp(scores - jnp.max(scores, axis=1, keepdims=True))
            chance = (grown / jnp.sum(grown, axis=1, keepdims=True)).astype(jnp.bfloat16)
            attention[tile:reach, span] = jnp.dot(
                chance, values[:reach, :], preferred_element_type=jnp.float32
            ).astype(jnp.bfloat16)

    prompt(0)
    for copy in sums:
        copy.wait_recv()
    tops, masses = [], []
    for head in range(2):
        top = parts_in[:, :, 2 * HD + head : 2 * HD + head + 1]
        mass = parts_in[:, :, 2 * HD + 2 + head : 2 * HD + 3 + head]
        highest = jnp.max(top, axis=0)
        factor = jnp.exp(top - highest[None])
        span = pl.ds(head * HD, HD)
        reply[:, span] = jnp.sum(parts_in[:, :, span] * factor, axis=0)
        tops.append(highest)
        masses.append(jnp.sum(mass * factor, axis=0))
    reply[:, 2 * HD :] = stats_of(tops, masses, lane[:8])
    replies[row] = reply[...]
    backs = [go(reply, replies.at[row], 52 + o, along_row(o)) for o in range(1, 16)]
    prompt(1)
    for copy in backs:
        copy.wait_recv()
    mine = jnp.where(holders[...] == lax.broadcasted_iota(jnp.int32, (8, 128), 1), 1.0, 0.0)
    got = jnp.dot(
        mine,
        replies[...].reshape(128, PACK),
        preferred_element_type=jnp.float32,
        precision=lax.Precision.HIGHEST,
    )
    own_key = keys[:16, :].astype(jnp.float32)[:8]
    own_value = values[:16, :].astype(jnp.float32)[:8]
    for head in range(2):
        span = pl.ds(head * HD, HD)
        own = SCALE * jnp.sum(own_query[:, span] * own_key, axis=1, keepdims=True)
        top = got[:, 2 * HD + head : 2 * HD + head + 1]
        mass = got[:, 2 * HD + 2 + head : 2 * HD + 3 + head]
        highest = jnp.maximum(top, own)
        theirs = jnp.exp(top - highest)
        ours = jnp.exp(own - highest)
        result = (got[:, head * HD : (head + 1) * HD] * theirs + own_value * ours) / (mass * theirs + ours)
        result = jnp.concatenate([result, result], axis=0)
        decoded = lax.broadcasted_iota(jnp.int32, (16, HD), 0) < 8
        attention[:16, span] = jnp.where(
            decoded, result, attention[:16, span].astype(jnp.float32)
        ).astype(jnp.bfloat16)
    return started


def layer_kernel(
    far_context, far_out, far_residual, gain_post, routes, scores, far_gate, far_up, far_down, table,
    gain_input, far_query, far_keyval, far_cosine, far_sine, segment_column, segment_row, holders,
    far_keys, far_values, share, new_cache, attention, context, w_out, residual, w_gate, w_up, w_down,
    w_query, w_keyval, cosine, sine, cache_keys, cache_values, normed, full, mid, tables, *rest,
):
    first_ring, second_ring, rest = rest[:7], rest[7:14], rest[14:]
    exchange, rest = rest[:8], rest[8:]
    heads, (fetched, *sems) = rest[:13], rest[13:]
    near = (context, w_out, residual, w_gate, w_up, w_down)
    near = near + (w_query, w_keyval, cosine, sine, cache_keys, cache_values)
    far = (far_context, far_out, far_residual, far_gate, far_up, far_down)
    far = far + (far_query, far_keyval, far_cosine, far_sine, far_keys, far_values)
    fetches = fetch(zip(far, near), fetched)
    peers = [along_row(o) for o in range(1, 16)] + [along_col(o) for o in range(1, 16)]
    peers = peers + [partner(o, 1) for o in range(8, 16)]
    barrier = greet(peers)
    for copy in fetches[:3]:
        copy.wait()
    started = project(
        context, w_out, residual, gain_post, normed, mid, first_ring[0], first_ring[1:], *sems[:2],
        lambda: pl.semaphore_wait(barrier, len(peers)),
    )
    started = started + apply_experts(
        normed, routes, scores, w_gate, w_up, w_down, fetches[3:6], mid, table, full, share, tables,
        second_ring[0], second_ring[1:], *exchange, *sems[2:4],
    )
    started = started + attend(
        full, gain_input, w_query, w_keyval, cosine, sine, fetches[6:], segment_column, segment_row,
        holders, tables, cache_keys, cache_values, new_cache, attention, *heads, *sems[4:],
    )
    for copy in started:
        copy.wait_send()


def layer(*operands):
    vmem = pl.BlockSpec(memory_space=pltpu.VMEM)
    far = pl.BlockSpec(memory_space=pltpu.HBM)
    f32, bf16, i32 = jnp.float32, jnp.bfloat16, jnp.int32
    chunks = pltpu.VMEM((16, CAP, D), bf16)
    counts = (2 * RING_SEMS, TABLE_SEMS + 16, 68)
    return pl.pallas_call(
        layer_kernel,
        out_shape=(
            jax.ShapeDtypeStruct((ROWS, 128), bf16),
            jax.ShapeDtypeStruct((ROWS, 64), bf16),
            jax.ShapeDtypeStruct((ROWS, 2 * HD), bf16),
        ),
        in_specs=[far] * 3 + [vmem] * 3 + [far] * 3 + [vmem] * 2 + [far] * 4 + [vmem] * 3 + [far] * 2,
        out_specs=(vmem,) * 3,
        scratch_shapes=[
            pltpu.VMEM((ROWS, 2 * HD), bf16),
            pltpu.VMEM((2 * HD, D), bf16),
            pltpu.VMEM((ROWS, 128), bf16),
            pltpu.VMEM((D, 384), bf16),
            pltpu.VMEM((D, 384), bf16),
            pltpu.VMEM((384, D), bf16),
            pltpu.VMEM((D, 2 * HD), bf16),
            pltpu.VMEM((D, 64), bf16),
            pltpu.VMEM((ROWS, HD), f32),
            pltpu.VMEM((ROWS, HD), f32),
            pltpu.VMEM((8, 64, 4 * HD), bf16),
            pltpu.VMEM((8, 64, 4 * HD), bf16),
            pltpu.VMEM((8, 2, BLOCK, D), bf16),
            pltpu.VMEM((8, 2, BLOCK, D), bf16),
            pltpu.VMEM((BLOCK, D), bf16),
            pltpu.VMEM((8, 128), i32),
        ]
        + ring_scratch()
        + ring_scratch()
        + [
            chunks,
            chunks,
            chunks,
            chunks,
            pltpu.VMEM((16, CAP, HALF_D), bf16),
            pltpu.VMEM((ROWS, D), f32),
            pltpu.VMEM((16 * CAP, ROWS), bf16),
            pltpu.VMEM((16, 8, 128), i32),
            pltpu.VMEM((ROWS, D), bf16),
            pltpu.VMEM((ROWS, 2 * HD), bf16),
            pltpu.VMEM((4, ROWS // 2, HD), bf16),
            pltpu.VMEM((ROWS, HD), bf16),
            pltpu.VMEM((ROWS, HD), bf16),
            pltpu.VMEM((8, 2 * HD), f32),
            pltpu.VMEM((16, 8, 2 * HD), f32),
            pltpu.VMEM((8, 2 * HD), f32),
            pltpu.VMEM((16, 8, 2 * HD), f32),
            pltpu.VMEM((16, 8, PACK), f32),
            pltpu.VMEM((16, 8, PACK), f32),
            pltpu.VMEM((8, PACK), f32),
            pltpu.VMEM((16, 8, PACK), f32),
            pltpu.SemaphoreType.DMA((12,)),
        ]
        + [pltpu.SemaphoreType.DMA((count,)) for count in counts for _ in range(2)],
        compiler_params=pltpu.CompilerParams(
            collective_id=0, has_side_effects=True, vmem_limit_bytes=60 << 20
        ),
        name="layer",
    )(*operands)


def shards(
    attn_context,
    residual,
    w_out,
    gain_post,
    gain_input,
    routes,
    router_scores,
    w_gate,
    w_up,
    w_down,
    w_query,
    w_keyval,
    segment_ids,
    cache_lengths,
    holders,
    cache_keys,
    cache_values,
):
    row = lax.axis_index("row")
    segment = segment_ids[0]
    earlier = jnp.sum((segment[None, :] < segment[:, None]).astype(jnp.int32), axis=1)
    position = jnp.concatenate([cache_lengths, jnp.arange(segment.shape[0], dtype=jnp.int32) - earlier])
    indices = jnp.arange(HD // 2).astype(jnp.float32)
    angles = position.astype(jnp.float32)[:, None] * (ROPE_THETA ** (-2.0 * indices / HD))[None, :]
    cosine, sine = jnp.cos(angles), jnp.sin(angles)
    cosine = jnp.concatenate([cosine, cosine], axis=1)
    sine = jnp.concatenate([-sine, sine], axis=1)
    segments = jnp.concatenate([jnp.full((8,), -1, jnp.int32), segment])
    table = jnp.stack([holders, cache_lengths])
    table = jnp.pad(table, ((0, 6), (0, 0)))
    table = jnp.where(
        jnp.arange(128, dtype=jnp.int32)[None, :] // 8 == row, jnp.tile(table, (1, 16)), 0
    )
    return layer(
        attn_context,
        w_out,
        residual,
        gain_post.reshape(1, D),
        routes.T,
        router_scores.T,
        w_gate[0],
        w_up[0],
        w_down[0],
        table,
        gain_input.reshape(1, D),
        w_query,
        w_keyval,
        cosine,
        sine,
        segments.reshape(ROWS, 1),
        segments.reshape(1, ROWS),
        holders.reshape(8, 1),
        cache_keys,
        cache_values,
    )


def solution(mesh):
    return jax.shard_map(
        shards,
        mesh=mesh,
        in_specs=(
            P("row", "col"),
            P("row", "col"),
            P("col", None),
            P(),
            P(),
            P("row", None),
            P("row", None),
            P(("row", "col"), None, None),
            P(("row", "col"), None, None),
            P(("row", "col"), None, None),
            P(None, "col"),
            P(None, "col"),
            P("row", None),
            P("row"),
            P("row"),
            P("row", "col", None),
            P("row", "col", None),
        ),
        out_specs=(P("row", "col"), P("row", "col"), P("row", "col")),
        check_vma=False,
    )
```

```python
import functools

import jax
import jax.numpy as jnp
from jax import lax
from jax.experimental import pallas as pl
from jax.experimental.pallas import tpu as pltpu
from jax.sharding import PartitionSpec as P

TOP = 8
QH = 32
KVH = 4
HD = 128
EPSILON = 1e-06
ROPE_THETA = 1000000.0
NEGATIVE = -1e30
MESH = pl.DeviceIdType.MESH

D = 2048
HALF_D = 1024
LEFT = pl.ds(0, HALF_D)
RIGHT = pl.ds(HALF_D, HALF_D)
ROWS = 512
BLOCK = 32
CAP = 64
RING_SEMS = 23
TILE = 512


def remote(src, dst, send, recv, index, device):
    return pltpu.make_async_remote_copy(
        src_ref=src,
        dst_ref=dst,
        send_sem=send.at[index],
        recv_sem=recv.at[index],
        device_id=device,
        device_id_type=MESH,
    )


def around():
    row = lax.axis_index("row")
    col = lax.axis_index("col")
    z = col // 2
    y = lax.rem(col, 2)
    after = (row, lax.rem(z + 1, 8) * 2 + y)
    before = (row, lax.rem(z + 7, 8) * 2 + y)
    beside = (row, z * 2 + 1 - y)
    return z, y, after, before, beside


def reduce_blocks(place, blocks, y_left, up_left, down_left, up_right, down_right, y_right, send, recv, base):
    z, y, after, before, beside = place
    other = 1 - y
    started = []

    def go(src, dst, index, device):
        copy = remote(src, dst, send, recv, base + index, device)
        copy.start()
        started.append(copy)
        return copy

    def at(offset):
        return lax.rem(z + offset + 8, 8)

    crossing = {}
    for index, offset in enumerate((4, -3, 3, -2, 2, -1, 1, 0)):
        t = at(offset)
        crossing[offset] = go(blocks.at[other, t, :, LEFT], y_left.at[t], index, beside)
    up_l, down_l, up_r, down_r = [], [], [], []
    for step in range(4):
        if step < 3:
            t = at(3 - step)
            if step:
                up_r[-1].wait_recv()
                blocks[:, t, :, RIGHT] = (
                    blocks[:, t, :, RIGHT].astype(jnp.float32) + up_right[step - 1].astype(jnp.float32)
                ).astype(jnp.bfloat16)
            up_r.append(go(blocks.at[:, t, :, RIGHT], up_right.at[step], 8 + step, after))
        t = at(step - 4)
        if step:
            down_r[-1].wait_recv()
            blocks[:, t, :, RIGHT] = (
                blocks[:, t, :, RIGHT].astype(jnp.float32) + down_right[step - 1].astype(jnp.float32)
            ).astype(jnp.bfloat16)
        down_r.append(go(blocks.at[:, t, :, RIGHT], down_right.at[step], 11 + step, before))
        t = at(4 - step)
        crossing[4 - step].wait_recv()
        value = blocks[y, t, :, LEFT].astype(jnp.float32) + y_left[t].astype(jnp.float32)
        if step:
            up_l[-1].wait_recv()
            value = value + up_left[step - 1].astype(jnp.float32)
        blocks[y, t, :, LEFT] = value.astype(jnp.bfloat16)
        up_l.append(go(blocks.at[y, t, :, LEFT], up_left.at[step], 15 + step, after))
        if step < 3:
            t = at(step - 3)
            crossing[step - 3].wait_recv()
            value = blocks[y, t, :, LEFT].astype(jnp.float32) + y_left[t].astype(jnp.float32)
            if step:
                down_l[-1].wait_recv()
                value = value + down_left[step - 1].astype(jnp.float32)
            blocks[y, t, :, LEFT] = value.astype(jnp.bfloat16)
            down_l.append(go(blocks.at[y, t, :, LEFT], down_left.at[step], 19 + step, before))
    up_r[-1].wait_recv()
    down_r[-1].wait_recv()
    blocks[other, z, :, RIGHT] = (
        blocks[other, z, :, RIGHT].astype(jnp.float32)
        + up_right[2, other].astype(jnp.float32)
        + down_right[3, other].astype(jnp.float32)
    ).astype(jnp.bfloat16)
    last = go(blocks.at[other, z, :, RIGHT], y_right, 22, beside)
    right = (
        blocks[y, z, :, RIGHT].astype(jnp.float32)
        + up_right[2, y].astype(jnp.float32)
        + down_right[3, y].astype(jnp.float32)
    )
    crossing[0].wait_recv()
    up_l[-1].wait_recv()
    down_l[-1].wait_recv()
    left = (
        blocks[y, z, :, LEFT].astype(jnp.float32)
        + y_left[z].astype(jnp.float32)
        + up_left[3].astype(jnp.float32)
        + down_left[2].astype(jnp.float32)
    )
    last.wait_recv()
    right = right + y_right[...].astype(jnp.float32)
    return left, right, started


def gather_blocks(place, full, send, recv, base):
    z, y, after, before, beside = place
    started = []

    def go(view, index, device):
        copy = remote(view, view, send, recv, base + index, device)
        copy.start()
        started.append(copy)
        return copy

    def at(offset):
        return lax.rem(z + offset + 8, 8)

    first = go(full.at[z, y, :, RIGHT], 0, beside)
    crossing = []
    up_l, down_l, up_r, down_r = [], [], [], []

    def cross(t):
        crossing.append(go(full.at[t, y, :, LEFT], 1 + len(crossing), beside))

    for step in range(4):
        if step:
            up_l[-1].wait_recv()
        up_l.append(go(full.at[at(-step), y, :, LEFT], 9 + step, after))
        if step < 3:
            if step:
                down_l[-1].wait_recv()
            down_l.append(go(full.at[at(step), y, :, LEFT], 13 + step, before))
        if step == 0:
            first.wait_recv()
        if step < 3:
            if step:
                up_r[-1].wait_recv()
            up_r.append(go(full.at[at(-step), :, :, RIGHT], 16 + step, after))
        if step:
            down_r[-1].wait_recv()
        down_r.append(go(full.at[at(step), :, :, RIGHT], 19 + step, before))
        cross(at(-step))
        if 0 < step < 3:
            cross(at(step))
    down_l[-1].wait_recv()
    cross(at(3))
    up_l[-1].wait_recv()
    cross(at(-4))
    up_r[-1].wait_recv()
    down_r[-1].wait_recv()
    for copy in crossing:
        copy.wait_recv()
    return started


def ring_scratch():
    return [
        pltpu.VMEM((2, 8, BLOCK, D), jnp.bfloat16),
        pltpu.VMEM((8, BLOCK, HALF_D), jnp.bfloat16),
        pltpu.VMEM((4, BLOCK, HALF_D), jnp.bfloat16),
        pltpu.VMEM((3, BLOCK, HALF_D), jnp.bfloat16),
        pltpu.VMEM((3, 2, BLOCK, HALF_D), jnp.bfloat16),
        pltpu.VMEM((4, 2, BLOCK, HALF_D), jnp.bfloat16),
        pltpu.VMEM((BLOCK, HALF_D), jnp.bfloat16),
    ]


def greet(devices):
    barrier = pltpu.get_barrier_semaphore()
    for device in devices:
        pl.semaphore_signal(barrier, inc=1, device_id=device, device_id_type=MESH)
    return barrier


def by_block(value):
    return value.reshape(8, 2, BLOCK, value.shape[-1])


def fetch(pairs, sems):
    copies = [pltpu.make_async_copy(far, near, sems.at[index]) for index, (far, near) in enumerate(pairs)]
    for copy in copies:
        copy.start()
    return copies


def project(context, w_out, residual, gain, normed, mid, blocks, buffers, send, recv, wait_for_all):
    place = around()
    z, y = place[:2]
    for tile in range(0, D, TILE):
        columns = pl.ds(tile, TILE)
        value = by_block(
            jnp.dot(context[...], w_out[:, columns], preferred_element_type=jnp.float32).astype(jnp.bfloat16)
        )
        blocks[0, :, :, columns] = value[:, 0]
        blocks[1, :, :, columns] = value[:, 1]
    own = pl.ds(pl.multiple_of((z * 2 + y) * 128, 128), 128)
    value = jnp.dot(context[...], w_out[:, own], preferred_element_type=jnp.float32)
    value = by_block((value + residual[...].astype(jnp.float32)).astype(jnp.bfloat16))
    blocks[0, :, :, own] = value[:, 0]
    blocks[1, :, :, own] = value[:, 1]
    wait_for_all()
    left, right, started = reduce_blocks(place, blocks, *buffers, send, recv, 0)
    left = left.astype(jnp.bfloat16)
    right = right.astype(jnp.bfloat16)
    mid[:, :HALF_D] = left
    mid[:, HALF_D:] = right
    left = left.astype(jnp.float32)
    right = right.astype(jnp.float32)
    mean = (
        jnp.sum(left * left, axis=-1, keepdims=True) + jnp.sum(right * right, axis=-1, keepdims=True)
    ) * (1.0 / D)
    inverse = lax.rsqrt(mean + EPSILON)
    gains = gain[...].astype(jnp.float32)
    normed[z, y, :, LEFT] = (left * inverse * gains[:, :HALF_D]).astype(jnp.bfloat16)
    normed[z, y, :, RIGHT] = (right * inverse * gains[:, HALF_D:]).astype(jnp.bfloat16)
    return started + gather_blocks(place, normed, send, recv, RING_SEMS)


SPLIT = (4, 5, 10, 11, 12, 13, 14, 15)
SENDS = (12, 14, 2, 10, 4, 6, 8, 0)
PLAN = (
    ('pass', (12, 13, 14, 15)),
    ('work', (0,)),
    ('pass', (10, 11)),
    ('work', (12,)),
    ('pass', (4, 5)),
    ('work', (8,)),
    ('give', (12, 13, 14, 15)),
    ('work', (4,)),
    ('give', (10, 11, 4, 5)),
)
WHOLE_RUNS = ((0, 4), (6, 10))
SPLIT_RUNS = ((10, 12), (12, 16), (4, 6))
SHARE_SEMS = 32
SWAP_SEMS = 48
RING_BASE = 64
TABLE_SEMS = RING_BASE + 2 * RING_SEMS


def partner(o, sign):
    row = lax.axis_index("row")
    col = lax.axis_index("col")
    z, y = col // 2, lax.rem(col, 2)
    yh, x, core = row // 8, lax.rem(row // 2, 4), lax.rem(row, 2)
    a, b, d = o // 8, (o // 2) % 4, o % 2
    there = lax.rem(yh + a, 2) * 8 + lax.rem(x + sign * b + 4, 4) * 2 + lax.rem(core + d, 2)
    return (there, z * 2 + lax.rem(y + a, 2))


def apply_experts(
    normed, routes, scores, w_gate, w_up, w_down, fetches, mid, table, full, share, tables,
    blocks, buffers, going, coming, result, back, swapped, total, weights, listed, send, recv,
):
    row = lax.axis_index("row")
    place = around()
    z, y, after, before, beside = place
    yh, x, core = row // 8, lax.rem(row // 2, 4), lax.rem(row, 2)

    offsets = lax.broadcasted_iota(jnp.int32, (16, 1), 0)
    a, b, d = offsets // 8, lax.rem(offsets // 2, 4), lax.rem(offsets, 2)
    expert = (
        lax.rem(yh + a, 2) * 8 + lax.rem(x + b, 4) * 2 + lax.rem(core + d, 2)
    ) * 8 + z
    score = scores[...]
    share_of = score / jnp.sum(score, axis=0, keepdims=True)
    hit = jnp.zeros((16, ROWS), jnp.float32)
    weight = jnp.zeros((16, ROWS), jnp.float32)
    for choice in range(TOP):
        match = routes[choice : choice + 1, :] == expert
        hit = hit + jnp.where(match, 1.0, 0.0)
        weight = weight + jnp.where(match, share_of[choice : choice + 1, :], 0.0)
    earlier = lax.broadcasted_iota(jnp.int32, (ROWS, ROWS), 0) < lax.broadcasted_iota(
        jnp.int32, (ROWS, ROWS), 1
    )
    rank = jnp.dot(
        hit.astype(jnp.bfloat16),
        jnp.where(earlier, 1.0, 0.0).astype(jnp.bfloat16),
        preferred_element_type=jnp.float32,
    )
    rank = jnp.where(hit > 0.0, rank, -1.0).astype(jnp.int32)
    slots = lax.broadcasted_iota(jnp.int32, (CAP, ROWS), 0)
    mine = y * HALF_D
    theirs = HALF_D - mine

    def half(start):
        return pl.ds(pl.multiple_of(start, HALF_D), HALF_D)

    def piece(start, tile):
        return pl.ds(pl.multiple_of(start + tile, TILE), TILE)

    started = []

    def go(src, dst, index, device):
        copy = remote(src, dst, send, recv, index, device)
        copy.start()
        started.append(copy)
        return copy

    def choose(chunks):
        picks = []
        for o in chunks:
            chosen = slots == rank[o : o + 1, :]
            picks.append(jnp.where(chosen, 1.0, 0.0).astype(jnp.bfloat16))
            weights[o * CAP : (o + 1) * CAP, :] = jnp.where(chosen, weight[o : o + 1, :], 0.0).astype(
                jnp.bfloat16
            )
        return jnp.concatenate(picks, axis=0)

    arrivals = {}
    for low in SENDS:
        pick = choose((low, low + 1))
        for tile in range(0, HALF_D if low in SPLIT else D, TILE):
            columns = piece(mine, tile) if low in SPLIT else pl.ds(tile, TILE)
            rows = normed[:, :, :, columns].reshape(ROWS, TILE)
            value = jnp.dot(pick, rows, preferred_element_type=jnp.float32)
            value = value.astype(jnp.bfloat16).reshape(2, CAP, TILE)
            if low:
                going[low : low + 2, :, columns] = value
            else:
                coming[0, :, columns] = value[0]
                going[1, :, columns] = value[1]
        for o in (low, low + 1):
            if o in SPLIT:
                arrivals[o] = go(going.at[o, :, half(mine)], coming.at[o, :, half(mine)], o, partner(o, 1))
            elif o:
                arrivals[o] = go(going.at[o], coming.at[o], o, partner(o, 1))
    lists = [go(table, listed.at[o], TABLE_SEMS + o, partner(o, 1)) for o in range(1, 16)]
    shared = {}

    def pass_on(o):
        columns = half(theirs if o >= 8 else mine)
        arrivals[o].wait_recv()
        shared[o] = go(coming.at[o, :, columns], coming.at[o, :, columns], SHARE_SEMS + o, beside)

    returns, swaps = {}, {}

    def work(group):
        for o in range(group, group + 4):
            if o in SPLIT:
                shared[o].wait_recv()
            elif o:
                arrivals[o].wait_recv()
        rows = coming[group : group + 4].reshape(4 * CAP, D)
        gate = jnp.dot(rows, w_gate[...], preferred_element_type=jnp.float32)
        up = jnp.dot(rows, w_up[...], preferred_element_type=jnp.float32)
        inner = (gate / (1.0 + jnp.exp(-gate)) * up).astype(jnp.bfloat16)
        for tile in range(0, D, TILE):
            columns = pl.ds(tile, TILE)
            value = jnp.dot(inner, w_down[:, columns], preferred_element_type=jnp.float32)
            result[group : group + 4, :, columns] = value.astype(jnp.bfloat16).reshape(4, CAP, TILE)
        for o in range(group, group + 4):
            if o in SPLIT:
                columns = half(mine if o >= 8 else theirs)
                swaps[o] = go(result.at[o, :, columns], swapped.at[o], SWAP_SEMS + o, beside)
            elif o:
                returns[o] = go(result.at[o], back.at[o], 16 + o, partner(o, -1))

    def give(o):
        columns = half(theirs if o >= 8 else mine)
        swaps[o].wait_recv()
        result[o, :, columns] = (
            result[o, :, columns].astype(jnp.float32) + swapped[o].astype(jnp.float32)
        ).astype(jnp.bfloat16)
        returns[o] = go(result.at[o, :, columns], back.at[o, :, columns], 16 + o, partner(o, -1))

    for copy in fetches:
        copy.wait()
    for task, chunks in PLAN:
        for o in chunks:
            {"pass": pass_on, "work": work, "give": give}[task](o)
    back[0] = result[0]
    for copy in lists:
        copy.wait_recv()
    known = table[...]
    for o in range(1, 16):
        known = known + listed[o]
    tables[...] = known

    def combine(low, high, columns):
        count = (high - low) * CAP
        return lax.dot_general(
            weights[low * CAP : high * CAP, :],
            back[low:high, :, columns].reshape(count, TILE),
            (((0,), (0,)), ((), ())),
            preferred_element_type=jnp.float32,
        )

    for low, high in WHOLE_RUNS:
        for o in range(max(low, 1), high):
            returns[o].wait_recv()
        for tile in range(0, D, TILE):
            columns = pl.ds(tile, TILE)
            value = combine(low, high, columns)
            total[:, columns] = value if low == 0 else total[:, columns] + value

    def settle(columns, value):
        value = by_block(value.astype(jnp.bfloat16))
        blocks[0, :, :, columns] = value[:, 0]
        blocks[1, :, :, columns] = value[:, 1]

    for tile in range(0, HALF_D, TILE):
        columns = piece(theirs, tile)
        settle(columns, total[:, columns])
    for low, high in SPLIT_RUNS:
        for o in range(low, high):
            returns[o].wait_recv()
        for tile in range(0, HALF_D, TILE):
            columns = piece(mine, tile)
            value = total[:, columns] + combine(low, high, columns)
            if (low, high) == SPLIT_RUNS[-1]:
                settle(columns, value)
            else:
                total[:, columns] = value
    left, right, ring = reduce_blocks(
        place, blocks, *buffers, send, recv, RING_BASE
    )
    full[z, y, :, LEFT] = (mid[:, :HALF_D].astype(jnp.float32) + left).astype(jnp.bfloat16)
    full[z, y, :, RIGHT] = (mid[:, HALF_D:].astype(jnp.float32) + right).astype(jnp.bfloat16)
    started = started + ring + gather_blocks(place, full, send, recv, RING_BASE + RING_SEMS)
    own = pl.ds(pl.multiple_of((z * 2 + y) * 128, 128), 128)
    share[...] = full[:, :, :, own].reshape(ROWS, 128)
    return started


SCALE = HD ** (-0.5)
PACK = 384


def turn(value, cosine, sine):
    return value * cosine + pltpu.roll(value, HD // 2, value.ndim - 1) * sine


def stats_of(top, mass, lane):
    return jnp.where(
        lane == 0, top[0], jnp.where(lane == 1, top[1], jnp.where(lane == 2, mass[0], mass[1]))
    )


def along_row(o):
    return (lax.rem(lax.axis_index("row") + o, 16), lax.axis_index("col"))


def along_col(o):
    return (lax.axis_index("row"), lax.rem(lax.axis_index("col") + o, 16))


def attend(
    full, gain, w_query, w_keyval, cosine, sine, fetches, segment_column, segment_row, holders, tables,
    cache_keys, cache_values, new_cache, attention,
    x_in, query, pieces, keys, values, own_query, all_query, slot_query, slots_query,
    parts, parts_in, reply, replies, send, recv,
):
    row = lax.axis_index("row")
    col = lax.axis_index("col")
    quarter = lax.rem(col, 4)
    first = col - quarter

    started = []

    def go(src, dst, index, device):
        copy = remote(src, dst, send, recv, index, device)
        copy.start()
        started.append(copy)
        return copy

    gains = gain[...].astype(jnp.float32)

    def norm(value):
        value = value.astype(jnp.float32)
        inverse = lax.rsqrt(jnp.mean(value * value, axis=-1, keepdims=True) + EPSILON)
        return (value * inverse * gains).astype(jnp.bfloat16)

    for copy in fetches:
        copy.wait()
    early = jnp.dot(norm(full[0, 0, :16, :]), w_query[...], preferred_element_type=jnp.float32)
    early = early.astype(jnp.bfloat16).astype(jnp.float32)
    for head in range(2):
        span = pl.ds(head * HD, HD)
        turned = turn(early[:, head * HD : (head + 1) * HD], cosine[:16, :], sine[:16, :])
        own_query[:, span] = turned.astype(jnp.bfloat16).astype(jnp.float32)[:8]
    all_query[row] = own_query[...]
    asks = [go(own_query, all_query.at[row], o, along_row(o)) for o in range(1, 16)]
    for tile in range(0, ROWS, 64):
        x_in[tile : tile + 64, :] = norm(full[tile // 64].reshape(64, D))
    keyval = lax.dot_general(
        x_in[...], w_keyval[...], (((1,), (1,)), ((), ())), preferred_element_type=jnp.float32
    ).astype(jnp.bfloat16)
    pieces[quarter] = jnp.concatenate([keyval[: ROWS // 2], keyval[ROWS // 2 :]], axis=1)
    shares = [
        go(pieces.at[quarter], pieces.at[quarter], 16 + o, (row, first + lax.rem(quarter + o, 4)))
        for o in range(1, 4)
    ]
    for copy in asks:
        copy.wait_recv()
    held = (
        tables[0:1, :] == row * 8 + lax.broadcasted_iota(jnp.int32, (8, 128), 0)
    )
    length = jnp.sum(jnp.where(held, tables[1:2, :], 0), axis=1, keepdims=True)
    slot_query[...] = jnp.dot(
        jnp.where(held, 1.0, 0.0).astype(jnp.bfloat16),
        all_query[...].reshape(128, 2 * HD).astype(jnp.bfloat16),
        preferred_element_type=jnp.float32,
    )
    slots_query[col] = slot_query[...]
    tells = [go(slot_query, slots_query.at[col], 20 + o, along_col(o)) for o in range(1, 16)]
    for head in range(2):
        span = pl.ds(head * HD, HD)
        value = jnp.dot(x_in[...], w_query[:, span], preferred_element_type=jnp.float32)
        value = value.astype(jnp.bfloat16).astype(jnp.float32)
        query[:, span] = turn(value, cosine[...], sine[...]).astype(jnp.bfloat16)
    for copy in tells:
        copy.wait_recv()
    group = lax.rem(lax.broadcasted_iota(jnp.int32, (32, 4 * HD), 0), 16) // 4
    matched = group == lax.broadcasted_iota(jnp.int32, (32, 4 * HD), 1) // HD
    spot = col * 64 + lax.broadcasted_iota(jnp.int32, (32, 64), 1)
    lane = lax.broadcasted_iota(jnp.int32, (16, HD), 1)
    for slot in range(8):
        asked = slots_query[:, slot, :]
        asked = jnp.concatenate([asked[:, :HD], asked[:, HD:]], axis=0)
        asked = jnp.where(matched, jnp.concatenate([asked] * 4, axis=1), 0.0).astype(jnp.bfloat16)
        scores = SCALE * lax.dot_general(
            asked, cache_keys[slot], (((1,), (1,)), ((), ())), preferred_element_type=jnp.float32
        )
        valid = spot < length[slot : slot + 1, :]
        scores = jnp.where(valid, scores, NEGATIVE)
        top = jnp.max(scores, axis=1, keepdims=True)
        grown = jnp.where(valid, jnp.exp(scores - top), 0.0)
        mass = jnp.sum(grown, axis=1, keepdims=True)
        blend = jnp.dot(grown.astype(jnp.bfloat16), cache_values[slot], preferred_element_type=jnp.float32)
        blend = jnp.where(matched, blend, 0.0)
        blend = blend[:, :HD] + blend[:, HD : 2 * HD] + blend[:, 2 * HD : 3 * HD] + blend[:, 3 * HD :]
        parts[:, slot, :HD] = blend[:16]
        parts[:, slot, HD : 2 * HD] = blend[16:]
        parts[:, slot, 2 * HD :] = stats_of((top[:16], top[16:]), (mass[:16], mass[16:]), lane)
    parts_in[0] = parts[col]
    sums = [
        go(parts.at[lax.rem(col + o, 16)], parts_in.at[o], 36 + o, along_col(o)) for o in range(1, 16)
    ]
    for copy in shares:
        copy.wait_recv()

    def piece(index):
        value = pieces[index]
        return jnp.concatenate([value[:, : HD // 2], value[:, HD // 2 :]], axis=0)

    quarters = [piece(index) for index in range(4)]
    key = jnp.concatenate(quarters[:2], axis=1).astype(jnp.float32)
    keys[...] = turn(key, cosine[...], sine[...]).astype(jnp.bfloat16)
    values[...] = jnp.concatenate(quarters[2:], axis=1)
    new_cache[...] = jnp.where(
        quarter == 0,
        keys[:, : HD // 2],
        jnp.where(
            quarter == 1,
            keys[:, HD // 2 :],
            jnp.where(quarter == 2, values[:, : HD // 2], values[:, HD // 2 :]),
        ),
    )

    def prompt(head):
        span = pl.ds(head * HD, HD)
        for tile in range(0, ROWS, 128):
            reach = tile + 128
            scores = SCALE * lax.dot_general(
                query[tile:reach, span], keys[:reach, :], (((1,), (1,)), ((), ())),
                preferred_element_type=jnp.float32,
            )
            allowed = (segment_column[tile:reach, :] == segment_row[:, :reach]) & (
                lax.broadcasted_iota(jnp.int32, (128, reach), 1)
                <= lax.broadcasted_iota(jnp.int32, (128, reach), 0) + tile
            )
            scores = jnp.where(allowed, scores, NEGATIVE)
            grown = jnp.exp(scores - jnp.max(scores, axis=1, keepdims=True))
            chance = (grown / jnp.sum(grown, axis=1, keepdims=True)).astype(jnp.bfloat16)
            attention[tile:reach, span] = jnp.dot(
                chance, values[:reach, :], preferred_element_type=jnp.float32
            ).astype(jnp.bfloat16)

    prompt(0)
    for copy in sums:
        copy.wait_recv()
    tops, masses = [], []
    for head in range(2):
        top = parts_in[:, :, 2 * HD + head : 2 * HD + head + 1]
        mass = parts_in[:, :, 2 * HD + 2 + head : 2 * HD + 3 + head]
        highest = jnp.max(top, axis=0)
        factor = jnp.exp(top - highest[None])
        span = pl.ds(head * HD, HD)
        reply[:, span] = jnp.sum(parts_in[:, :, span] * factor, axis=0)
        tops.append(highest)
        masses.append(jnp.sum(mass * factor, axis=0))
    reply[:, 2 * HD :] = stats_of(tops, masses, lane[:8])
    replies[row] = reply[...]
    backs = [go(reply, replies.at[row], 52 + o, along_row(o)) for o in range(1, 16)]
    prompt(1)
    for copy in backs:
        copy.wait_recv()
    mine = jnp.where(holders[...] == lax.broadcasted_iota(jnp.int32, (8, 128), 1), 1.0, 0.0)
    got = jnp.dot(
        mine,
        replies[...].reshape(128, PACK),
        preferred_element_type=jnp.float32,
        precision=lax.Precision.HIGHEST,
    )
    own_key = keys[:16, :].astype(jnp.float32)[:8]
    own_value = values[:16, :].astype(jnp.float32)[:8]
    for head in range(2):
        span = pl.ds(head * HD, HD)
        own = SCALE * jnp.sum(own_query[:, span] * own_key, axis=1, keepdims=True)
        top = got[:, 2 * HD + head : 2 * HD + head + 1]
        mass = got[:, 2 * HD + 2 + head : 2 * HD + 3 + head]
        highest = jnp.maximum(top, own)
        theirs = jnp.exp(top - highest)
        ours = jnp.exp(own - highest)
        result = (got[:, head * HD : (head + 1) * HD] * theirs + own_value * ours) / (mass * theirs + ours)
        result = jnp.concatenate([result, result], axis=0)
        decoded = lax.broadcasted_iota(jnp.int32, (16, HD), 0) < 8
        attention[:16, span] = jnp.where(
            decoded, result, attention[:16, span].astype(jnp.float32)
        ).astype(jnp.bfloat16)
    return started


def layer_kernel(
    far_context, far_out, far_residual, gain_post, routes, scores, far_gate, far_up, far_down, table,
    gain_input, far_query, far_keyval, far_cosine, far_sine, segment_column, segment_row, holders,
    far_keys, far_values, packed, context, w_out, residual, w_gate, w_up, w_down,
    w_query, w_keyval, cosine, sine, cache_keys, cache_values, normed, full, mid, tables, *rest,
):
    first_ring, second_ring, rest = rest[:7], rest[7:14], rest[14:]
    exchange, rest = rest[:8], rest[8:]
    heads, (fetched, *sems) = rest[:13], rest[13:]
    share, attention, new_cache = packed.at[:, :128], packed.at[:, 128:384], packed.at[:, 384:448]
    near = (context, w_out, residual, w_gate, w_up, w_down)
    near = near + (w_query, w_keyval, cosine, sine, cache_keys, cache_values)
    far = (far_context, far_out, far_residual, far_gate, far_up, far_down)
    far = far + (far_query, far_keyval, far_cosine, far_sine, far_keys, far_values)
    fetches = fetch(zip(far, near), fetched)
    peers = [along_row(o) for o in range(1, 16)] + [along_col(o) for o in range(1, 16)]
    peers = peers + [partner(o, 1) for o in range(8, 16)]
    barrier = greet(peers)
    for copy in fetches[:3]:
        copy.wait()
    started = project(
        context, w_out, residual, gain_post, normed, mid, first_ring[0], first_ring[1:], *sems[:2],
        lambda: pl.semaphore_wait(barrier, len(peers)),
    )
    started = started + apply_experts(
        normed, routes, scores, w_gate, w_up, w_down, fetches[3:6], mid, table, full, share, tables,
        second_ring[0], second_ring[1:], *exchange, *sems[2:4],
    )
    started = started + attend(
        full, gain_input, w_query, w_keyval, cosine, sine, fetches[6:], segment_column, segment_row,
        holders, tables, cache_keys, cache_values, new_cache, attention, *heads, *sems[4:],
    )
    for copy in started:
        copy.wait_send()


def layer(*operands):
    vmem = pl.BlockSpec(memory_space=pltpu.VMEM)
    far = pl.BlockSpec(memory_space=pltpu.HBM)
    f32, bf16, i32 = jnp.float32, jnp.bfloat16, jnp.int32
    chunks = pltpu.VMEM((16, CAP, D), bf16)
    counts = (2 * RING_SEMS, TABLE_SEMS + 16, 68)
    return pl.pallas_call(
        layer_kernel,
        out_shape=jax.ShapeDtypeStruct((ROWS, 512), bf16),
        in_specs=[far] * 3 + [vmem] * 3 + [far] * 3 + [vmem] * 2 + [far] * 4 + [vmem] * 3 + [far] * 2,
        out_specs=vmem,
        scratch_shapes=[
            pltpu.VMEM((ROWS, 2 * HD), bf16),
            pltpu.VMEM((2 * HD, D), bf16),
            pltpu.VMEM((ROWS, 128), bf16),
            pltpu.VMEM((D, 384), bf16),
            pltpu.VMEM((D, 384), bf16),
            pltpu.VMEM((384, D), bf16),
            pltpu.VMEM((D, 2 * HD), bf16),
            pltpu.VMEM((64, D), bf16),
            pltpu.VMEM((ROWS, HD), f32),
            pltpu.VMEM((ROWS, HD), f32),
            pltpu.VMEM((8, 64, 4 * HD), bf16),
            pltpu.VMEM((8, 64, 4 * HD), bf16),
            pltpu.VMEM((8, 2, BLOCK, D), bf16),
            pltpu.VMEM((8, 2, BLOCK, D), bf16),
            pltpu.VMEM((BLOCK, D), bf16),
            pltpu.VMEM((8, 128), i32),
        ]
        + ring_scratch()
        + ring_scratch()
        + [
            chunks,
            chunks,
            chunks,
            chunks,
            pltpu.VMEM((16, CAP, HALF_D), bf16),
            pltpu.VMEM((ROWS, D), f32),
            pltpu.VMEM((16 * CAP, ROWS), bf16),
            pltpu.VMEM((16, 8, 128), i32),
            pltpu.VMEM((ROWS, D), bf16),
            pltpu.VMEM((ROWS, 2 * HD), bf16),
            pltpu.VMEM((4, ROWS // 2, HD), bf16),
            pltpu.VMEM((ROWS, HD), bf16),
            pltpu.VMEM((ROWS, HD), bf16),
            pltpu.VMEM((8, 2 * HD), f32),
            pltpu.VMEM((16, 8, 2 * HD), f32),
            pltpu.VMEM((8, 2 * HD), f32),
            pltpu.VMEM((16, 8, 2 * HD), f32),
            pltpu.VMEM((16, 8, PACK), f32),
            pltpu.VMEM((16, 8, PACK), f32),
            pltpu.VMEM((8, PACK), f32),
            pltpu.VMEM((16, 8, PACK), f32),
            pltpu.SemaphoreType.DMA((12,)),
        ]
        + [pltpu.SemaphoreType.DMA((count,)) for count in counts for _ in range(2)],
        compiler_params=pltpu.CompilerParams(
            collective_id=0, has_side_effects=True, vmem_limit_bytes=60 << 20
        ),
        name="layer",
    )(*operands)


def shards(
    attn_context,
    residual,
    w_out,
    gain_post,
    gain_input,
    routes,
    router_scores,
    w_gate,
    w_up,
    w_down,
    w_query,
    w_keyval,
    segment_ids,
    cache_lengths,
    holders,
    cache_keys,
    cache_values,
):
    row = lax.axis_index("row")
    segment = segment_ids[0]
    earlier = jnp.sum((segment[None, :] < segment[:, None]).astype(jnp.int32), axis=1)
    position = jnp.concatenate([cache_lengths, jnp.arange(segment.shape[0], dtype=jnp.int32) - earlier])
    indices = jnp.arange(HD // 2).astype(jnp.float32)
    angles = position.astype(jnp.float32)[:, None] * (ROPE_THETA ** (-2.0 * indices / HD))[None, :]
    cosine, sine = jnp.cos(angles), jnp.sin(angles)
    cosine = jnp.concatenate([cosine, cosine], axis=1)
    sine = jnp.concatenate([-sine, sine], axis=1)
    segments = jnp.concatenate([jnp.full((8,), -1, jnp.int32), segment])
    table = jnp.stack([holders, cache_lengths])
    table = jnp.pad(table, ((0, 6), (0, 0)))
    table = jnp.where(
        jnp.arange(128, dtype=jnp.int32)[None, :] // 8 == row, jnp.tile(table, (1, 16)), 0
    )
    packed = layer(
        attn_context,
        w_out,
        residual,
        gain_post.reshape(1, D),
        routes.T,
        router_scores.T,
        w_gate[0],
        w_up[0],
        w_down[0],
        table,
        gain_input.reshape(1, D),
        w_query,
        w_keyval.T,
        cosine,
        sine,
        segments.reshape(ROWS, 1),
        segments.reshape(1, ROWS),
        holders.reshape(8, 1),
        cache_keys,
        cache_values,
    )
    return (packed[:, :128], packed[:, 384:448], packed[:, 128:384])


def solution(mesh):
    return jax.shard_map(
        shards,
        mesh=mesh,
        in_specs=(
            P("row", "col"),
            P("row", "col"),
            P("col", None),
            P(),
            P(),
            P("row", None),
            P("row", None),
            P(("row", "col"), None, None),
            P(("row", "col"), None, None),
            P(("row", "col"), None, None),
            P(None, "col"),
            P(None, "col"),
            P("row", None),
            P("row"),
            P("row"),
            P("row", "col", None),
            P("row", "col", None),
        ),
        out_specs=(P("row", "col"), P("row", "col"), P("row", "col")),
        check_vma=False,
    )
```
